32 devices in a mesh: row: 4 (over z), col: 4 (over x, core), tm: 2 (over y).
Axes of the slice: x: 2, y: 2, z: 4, core: 2. Of those that a mesh axis runs over, the one named last changes fastest.
Arguments:
- samples: bfloat16 [1024, 4, 2, 16384], P('row', None, 'tm', 'col'), may hold values from -6 to 6
- whitening: bfloat16 [1024, 1024], replicated, may hold values from -0.1875 to 0.1875
- ridge: float32 [2048], P('col'), may hold values from 2 to 20
- slab_start: int32 [1], replicated, may hold values from 0 to 63
- panels: int32 [4], replicated, may hold values from 0 to 3, as said below
Outputs:
- trailing: float32 [131072, 2048], P(('row', 'tm'), 'col')
- factor: bfloat16 [2, 131072, 512], P(None, ('row', 'tm'))
The draws below stay inside these ranges and needn't reach their ends.
Inputs may be any that keep to these rules, and one draw needn't show every extreme that they name: `panels`: each panel index once.
All inputs are finite; a program needn't handle non-finite values.
Results may differ from the reference program's by a relative error of at most 0.012.
The reference program's roundings to bfloat16 on the way count: a program that leaves them out, or rounds other values in their place, can miss the bound.
Values may be sent and summed in bfloat16 or wider, within the bound.
A program may use at most 256 MiB of HBM per device.

```python
import math
import jax
import jax.numpy as jnp
from jax import lax

K = 131072
S = 1024
PANEL = 512
PANELS = 2
SLAB = 2048
KD = 16384
N_ROW = 4
N_COL = 4
N_TM = 2


def draw_panels(key, part):
    scored = jax.random.fold_in(key, 9173)
    scores = jax.random.randint(scored, (N_COL,), 0, 1 << 20) * N_COL + jnp.arange(N_COL, dtype=jnp.int32)
    return jnp.argsort(scores, stable=True).astype(jnp.int32)


def steps_of(stream_key, dims, cuts, low, largest):
    level, own = 1.0, jax.random.fold_in(stream_key, 6)
    for position, shards_of in cuts:
        steps = jnp.exp(jax.random.uniform(jax.random.fold_in(own, position), (shards_of,), jnp.float32, low / len(cuts), largest / len(cuts)))
        level = level * jnp.repeat(steps, dims[position] // shards_of).reshape([-1 if axis == position else 1 for axis in range(len(dims))])
    return level


def centred(key, shape, spread, bound, split=(), kind=jnp.bfloat16):
    level = steps_of(key, shape, split, -0.22, 0.18) if split else 1.0
    values = jax.random.normal(key, shape, jnp.float32) * spread * level
    return jnp.minimum(jnp.maximum(values, -bound), bound).astype(kind)


def setup_inputs(seed: int = 0) -> dict:
    keys = jax.random.split(jax.random.key(seed), 6)
    samples = centred(keys[0], (S, N_ROW, N_TM, KD), 1.0, 6.0, ((0, 4), (2, 2), (3, 4)))
    whitening = centred(keys[1], (S, S), S ** -0.5, 0.1875)
    ridge = jnp.clip(jnp.exp(math.log(20.0) - 2.3025851 * jax.random.uniform(keys[2], (SLAB,), jnp.float32) ** steps_of(keys[2], (SLAB,), ((0, 4),), -0.2, 0.2)), 2.0, 20.0)
    slab_start = jax.random.randint(keys[3], (1,), 0, K // SLAB).astype(jnp.int32)
    panels = draw_panels(jax.random.fold_in(keys[5], 71), 0)
    return {"samples": samples, "whitening": whitening, "ridge": ridge, "slab_start": slab_start, "panels": panels}


def reference(samples, whitening, ridge, slab_start, panels):
    flat_data = samples.reshape(S, K)
    whitened = jnp.dot(whitening.astype(jnp.float32), flat_data.astype(jnp.float32), preferred_element_type=jnp.float32).astype(jnp.bfloat16)
    slab_first = (slab_start[0] * SLAB).astype(jnp.int32)
    slab_data = lax.dynamic_slice_in_dim(whitened, slab_first, SLAB, 1)
    covariance = lax.dot_general(whitened.astype(jnp.float32), slab_data.astype(jnp.float32), (((0,), (0,)), ((), ())), preferred_element_type=jnp.float32) * (1.0 / math.sqrt(S))
    zero_index = jnp.zeros((), jnp.int32)
    diag_block = lax.dynamic_slice(covariance, (slab_first, zero_index), (SLAB, SLAB)) + jnp.diag(ridge)
    covariance = lax.dynamic_update_slice(covariance, diag_block, (slab_first, zero_index))
    factors = []
    for section in range(PANELS):
        panel_first = (panels[section] * PANEL).astype(jnp.int32)
        pivot_rows = lax.dynamic_slice_in_dim(covariance, slab_first + panel_first, PANEL, 0)
        pivot_diag = lax.dynamic_slice_in_dim(pivot_rows, panel_first, PANEL, 1)
        lower_factor = jnp.linalg.cholesky(pivot_diag)
        panel_columns = lax.dynamic_slice_in_dim(covariance, panel_first, PANEL, 1)
        panel_now = jax.scipy.linalg.solve_triangular(lower_factor, panel_columns.T, lower=True).T.astype(jnp.bfloat16)
        coupling = jax.scipy.linalg.solve_triangular(lower_factor, pivot_rows, lower=True).T.astype(jnp.bfloat16)
        covariance = covariance - lax.dot_general(panel_now.astype(jnp.float32), coupling.astype(jnp.float32), (((1,), (1,)), ((), ())), preferred_element_type=jnp.float32)
        factors.append(panel_now)
    column_panel = jnp.arange(SLAB) // PANEL
    finished = column_panel == panels[0]
    for section in range(1, PANELS):
        finished = finished | (column_panel == panels[section])
    trailing = jnp.where(finished[None, :], jnp.zeros((), covariance.dtype), covariance)
    return (trailing, jnp.stack(factors))
```

```python
import functools
import math
import jax
import jax.numpy as jnp
from jax import lax
from jax.experimental import pallas as pl
from jax.experimental.pallas import tpu as pltpu
from jax.sharding import PartitionSpec as P

NB = 128
SUB = 8
HIGH = lax.Precision.HIGHEST


def block_inverse(a):
    n = NB // SUB
    rows = [a[s * SUB:(s + 1) * SUB, :] for s in range(n)]
    lane = lax.broadcasted_iota(jnp.int32, (SUB, NB), 1)
    sub = lax.broadcasted_iota(jnp.int32, (SUB, NB), 0)
    inv = [jnp.where(lane == sub + s * SUB, 1.0, 0.0).astype(jnp.float32) for s in range(n)]
    for k in range(NB):
        s0, r = divmod(k, SUB)
        row_a = rows[s0][r:r + 1, :]
        row_v = inv[s0][r:r + 1, :]
        scale = 1.0 / row_a[:, k:k + 1]
        row_a_s = row_a * scale
        row_v_s = row_v * scale
        for s in range(s0, n):
            column = jnp.broadcast_to(rows[s][:, k:k + 1], (SUB, NB))
            if s == s0:
                if r == SUB - 1:
                    continue
                column = jnp.where(sub > r, column, 0.0)
            rows[s] = rows[s] - column * row_a_s
            inv[s] = inv[s] - column * row_v_s
    out = []
    for s in range(n):
        d = jnp.sum(jnp.where(lane == sub + s * SUB, rows[s], 0.0), axis=1, keepdims=True)
        out.append(inv[s] / jnp.sqrt(d))
    return jnp.concatenate(out, axis=0)


def inverse_kernel(a_ref, o_ref, work):
    size = a_ref.shape[0]
    work[:, :size] = a_ref[...]
    ri = lax.broadcasted_iota(jnp.int32, (size, size), 0)
    ci = lax.broadcasted_iota(jnp.int32, (size, size), 1)
    work[:, size:] = jnp.where(ri == ci, 1.0, 0.0).astype(jnp.float32)
    row_id = lax.broadcasted_iota(jnp.int32, (size, 1), 0)

    def step(b, carry):
        at = pl.multiple_of(b * NB, NB)
        small = block_inverse(work[pl.ds(at, NB), pl.ds(at, NB)])
        top = jnp.dot(small, work[pl.ds(at, NB), :], preferred_element_type=jnp.float32, precision=HIGH)
        left = jnp.where(row_id >= at + NB, top[:, :size].T, 0.0)
        update = jnp.dot(left, top, preferred_element_type=jnp.float32, precision=HIGH)
        work[...] = work[...] - update
        work[pl.ds(at, NB), :] = top
        return carry

    lax.fori_loop(0, size // NB, step, 0)
    o_ref[...] = work[:, size:]


def lower_inverse(a):
    size = a.shape[0]
    return pl.pallas_call(
        inverse_kernel,
        out_shape=jax.ShapeDtypeStruct((size, size), jnp.float32),
        in_specs=[pl.BlockSpec(memory_space=pltpu.VMEM)],
        out_specs=pl.BlockSpec(memory_space=pltpu.VMEM),
        scratch_shapes=[pltpu.VMEM((size, 2 * size), jnp.float32)],
        compiler_params=pltpu.CompilerParams(vmem_limit_bytes=40 * 2**20),
        cost_estimate=pl.CostEstimate(flops=30 * 10**9, bytes_accessed=2 * 2**20, transcendentals=0),
        name="lower_inverse",
    )(a)


def split_kernel(rows, info, x_ref, *outs):
    for k in range(rows):
        @pl.when(info[0] == k)
        def _():
            for s, o in enumerate(outs):
                o[...] = x_ref[:, (k + s) % rows, :]


def split_blocks(row, x, first, w):
    times, rows, _ = x.shape
    bt = min(64, times)
    return pl.pallas_call(
        functools.partial(split_kernel, rows),
        grid_spec=pltpu.PrefetchScalarGridSpec(
            num_scalar_prefetch=1,
            grid=(times // bt,),
            in_specs=[pl.BlockSpec((bt, rows, w), lambda i, info: (i, 0, first // w))],
            out_specs=[pl.BlockSpec((bt, w), lambda i, info: (i, 0))] * rows,
        ),
        out_shape=[jax.ShapeDtypeStruct((times, w), x.dtype)] * rows,
        cost_estimate=pl.CostEstimate(flops=0, bytes_accessed=4 * times * rows * w * 2, transcendentals=0),
        name="split_blocks",
    )(row, x)


def final_body(bm, chunk_base, n_x, info, *refs):
    xs, ms = refs[:n_x], refs[n_x:2 * n_x]
    d0_ref, d1_ref, dn_ref = refs[2 * n_x:2 * n_x + 3]
    t_ref, f_ref = refs[-2:]
    width = t_ref.shape[1]
    acc = None
    for x, m in zip(xs, ms):
        part = lax.dot_general(x[0], m[...], (((0,), (0,)), ((), ())), preferred_element_type=jnp.float32)
        acc = part if acc is None else acc + part
    block = chunk_base(pl.program_id(0), pl.program_id(1))
    inside = (block >= info[0]) & (block < info[1])

    @pl.when(inside)
    def _():
        f_ref[0] = (acc[:, :width] + d0_ref[...]).astype(f_ref.dtype)
        f_ref[1] = (acc[:, width:2 * width] + d1_ref[...]).astype(f_ref.dtype)
        t_ref[...] = acc[:, 2 * width:] + dn_ref[...]

    @pl.when(jnp.logical_not(inside))
    def _():
        f_ref[0] = acc[:, :width].astype(f_ref.dtype)
        f_ref[1] = acc[:, width:2 * width].astype(f_ref.dtype)
        t_ref[...] = acc[:, 2 * width:]


def final_chunk(info, own, others, weights, d0, d1, dn, prior, chunk, chunks, width, bm):
    cols, times, local = own.shape
    w = local // chunks
    per = w // bm
    rows = cols * local
    rest = others.shape[1]

    def base(c, i):
        return c * (local // bm) + chunk * per + i

    def d_map(c, i, info):
        block = base(c, i)
        inside = (block >= info[0]) & (block < info[1])
        return (jnp.where(inside, block - info[0], 0), 0)

    in_specs = [
        pl.BlockSpec((1, times, bm), lambda c, i, info: (c, 0, chunk * per + i)),
        pl.BlockSpec((1, rest, bm), lambda c, i, info: (c, 0, i)),
        pl.BlockSpec((times, 3 * width), lambda c, i, info: (0, 0)),
        pl.BlockSpec((rest, 3 * width), lambda c, i, info: (0, 0)),
        pl.BlockSpec((bm, width), d_map),
        pl.BlockSpec((bm, width), d_map),
        pl.BlockSpec((bm, width), d_map),
    ]
    operands = [info, own, others, weights[:times], weights[times:], d0, d1, dn]
    aliases = {}
    if prior is not None:
        in_specs += [pl.BlockSpec(memory_space=pl.ANY)] * 2
        aliases = {len(operands): 0, len(operands) + 1: 1}
        operands += list(prior)
    return pl.pallas_call(
        functools.partial(final_body, bm, base, 2),
        grid_spec=pltpu.PrefetchScalarGridSpec(
            num_scalar_prefetch=1,
            grid=(cols, per),
            in_specs=in_specs,
            out_specs=[
                pl.BlockSpec((bm, width), lambda c, i, info: (base(c, i), 0)),
                pl.BlockSpec((2, bm, width), lambda c, i, info: (0, base(c, i), 0)),
            ],
        ),
        out_shape=[
            jax.ShapeDtypeStruct((rows, width), jnp.float32),
            jax.ShapeDtypeStruct((2, rows, width), jnp.bfloat16),
        ],
        input_output_aliases=aliases,
        compiler_params=pltpu.CompilerParams(
            vmem_limit_bytes=48 * 2**20, dimension_semantics=("arbitrary", "arbitrary")
        ),
        cost_estimate=pl.CostEstimate(
            flops=2 * cols * w * (times + rest) * 3 * width, bytes_accessed=cols * w * 6 * 2**10, transcendentals=0),
        name="final",
    )(*operands)


def high(a, b, dims):
    return lax.dot_general(a, b, ((dims[:1], dims[1:]), ((), ())), preferred_element_type=jnp.float32, precision=HIGH)


def on_device(samples, whitening, ridge, slab_start, panels):
    times, groups, _, local = samples.shape
    rows = lax.axis_size("row")
    cols = lax.axis_size("col")
    tms = lax.axis_size("tm")
    width = ridge.shape[0]
    slab = width * cols
    kd = local * cols
    depth = whitening.shape[0]
    scale = 1.0 / math.sqrt(depth)
    me_col = lax.axis_index("col")
    me_tm = lax.axis_index("tm")
    me_row = lax.axis_index("row")

    first = slab_start[0] * slab
    group = first // (tms * kd)
    tm_owner = (first % (tms * kd)) // kd
    offset = first % kd

    mine = lax.dynamic_index_in_dim(samples[:, :, 0], group, 1, keepdims=False)
    pieces = []
    for p in range(cols):
        at = offset + p * width
        have = (me_tm == tm_owner) & (me_col == at // local)
        part = lax.dynamic_slice_in_dim(mine, at % local, width, 1)
        pieces.append(jnp.where(have, part, jnp.zeros_like(part)))
    raw = lax.psum(jnp.concatenate(pieces, axis=1), ("tm", "col"))
    raw = lax.all_gather(raw, "row", axis=0, tiled=True)
    ridge_all = lax.all_gather(ridge, "col", axis=0, tiled=True)

    chunks = 4 if local >= 4096 else 2
    w = local // chunks
    flat = samples.reshape(times, groups, local)
    row_info = me_row.reshape(1).astype(jnp.int32)
    own_parts, moved = [], []
    for c in range(chunks):
        blocks = split_blocks(row_info, flat, c * w, w)
        own_parts.append(blocks[0])
        moved.append([
            lax.ppermute(blocks[s], "row", [(i, (i + s) % rows) for i in range(rows)]) for s in range(1, rows)
        ])
    own = lax.all_gather(jnp.concatenate(own_parts, axis=1), "col", axis=0)
    others = [lax.all_gather(jnp.concatenate(m, axis=0), "col", axis=0) for m in moved]

    sw = jnp.dot(whitening, raw, preferred_element_type=jnp.float32).astype(jnp.bfloat16)
    cut = lambda q: lax.dynamic_slice_in_dim(sw, q * width, width, 1)
    q0, q1 = panels[0], panels[1]
    s0, s1, sj = cut(q0), cut(q1), cut(me_col)
    r0 = lax.dynamic_slice_in_dim(ridge_all, q0 * width, width, 0)
    r1 = lax.dynamic_slice_in_dim(ridge_all, q1 * width, width, 0)
    both = jnp.concatenate([s0, s1], axis=1)
    gram = lax.dot_general(
        both, jnp.concatenate([both, sj], axis=1), (((0,), (0,)), ((), ())), preferred_element_type=jnp.float32
    ) * scale
    own0 = (q0 == me_col).astype(jnp.float32)
    own1 = (q1 == me_col).astype(jnp.float32)
    a00 = gram[:width, :width] + jnp.diag(r0)
    a01 = gram[:width, width:2 * width]
    a0j = gram[:width, 2 * width:] + jnp.diag(r0) * own0
    a11 = gram[width:, width:2 * width] + jnp.diag(r1)
    a1j = gram[width:, 2 * width:] + jnp.diag(r1) * own1
    i0 = lower_inverse(a00)
    c0 = high(i0, jnp.concatenate([a01, a0j], axis=1), (1, 0)).astype(jnp.bfloat16)
    c01, c0j = c0[:, :width], c0[:, width:]
    fix = lax.dot_general(c01, c0, (((0,), (0,)), ((), ())), preferred_element_type=jnp.float32)
    i1 = lower_inverse(a11 - fix[:, :width])
    c1j = high(i1, a1j - fix[:, width:], (1, 0)).astype(jnp.bfloat16)

    zero = jnp.zeros((width, width), jnp.float32)
    e0 = jnp.diag(r0)
    e1 = jnp.diag(r1)
    m0 = high(jnp.concatenate([s0.astype(jnp.float32) * scale, e0], axis=0), i0, (1, 1))
    m0z = jnp.concatenate([m0, zero], axis=0)
    t1 = jnp.concatenate([s1.astype(jnp.float32) * scale, zero, e1], axis=0) - high(
        m0z, c01.astype(jnp.float32), (1, 0))
    m1 = high(t1, i1, (1, 1))
    base = jnp.concatenate([sj.astype(jnp.float32) * scale, zero, zero], axis=0)
    n = base - high(m0z, c0j.astype(jnp.float32), (1, 0)) - high(m1, c1j.astype(jnp.float32), (1, 0))
    finished = (me_col == q0) | (me_col == q1)
    n = jnp.where(finished, 0.0, n)
    weights = jnp.concatenate([m0[:depth], m1[:depth], n[:depth]], axis=1).astype(jnp.bfloat16)
    order = (me_row - jnp.arange(rows)) % rows
    turned = jnp.take(whitening.reshape(depth, rows, times), order, axis=1).reshape(depth, depth)
    weights = lax.dot_general(
        turned, weights, (((0,), (0,)), ((), ())), preferred_element_type=jnp.float32
    ).astype(jnp.bfloat16)

    def spread(rows):
        out = jnp.zeros((slab, width), jnp.float32)
        out = lax.dynamic_update_slice(out, rows[:width], (q0 * width, jnp.zeros((), jnp.int32)))
        return lax.dynamic_update_slice(out, rows[width:], (q1 * width, jnp.zeros((), jnp.int32)))

    d0 = spread(m0z[depth:])
    d1 = spread(m1[depth:])
    own_ridge = jnp.where(finished, 0.0, jnp.diag(ridge))
    dn = spread(n[depth:])
    zi = jnp.zeros((), jnp.int32)
    at = (me_col * width, zi)
    dn = lax.dynamic_update_slice(dn, lax.dynamic_slice(dn, at, (width, width)) + own_ridge, at)

    bm = min(512, w)
    owner = (me_row == group) & (me_tm == tm_owner)
    low_block = offset // bm
    info = jnp.stack([
        jnp.where(owner, low_block, 0),
        jnp.where(owner, low_block + slab // bm, 0),
    ]).astype(jnp.int32)
    prior = None
    for c in range(chunks):
        prior = final_chunk(info, own, others[c], weights, d0, d1, dn, prior, c, chunks, width, bm)
    return tuple(prior)


def solution(mesh):
    in_specs = (P("row", None, "tm", "col"), P(), P("col"), P(), P())
    out_specs = (P(("row", "tm"), "col"), P(None, ("row", "tm"), None))
    return jax.shard_map(
        on_device, mesh=mesh, in_specs=in_specs, out_specs=out_specs, check_vma=False
    )
```

```python
import functools
import math
import jax
import jax.numpy as jnp
from jax import lax
from jax.experimental import pallas as pl
from jax.experimental.pallas import tpu as pltpu
from jax.sharding import PartitionSpec as P

NB = 128
SUB = 8
HIGH = lax.Precision.HIGHEST
MESH = pl.DeviceIdType.MESH
NN = (((1,), (0,)), ((), ()))
NT = (((1,), (1,)), ((), ()))
TN = (((0,), (0,)), ((), ()))


def spread(x):
    return jnp.broadcast_to(x, (SUB, NB))


def block_inverse(a, held):
    n = NB // SUB
    rows = [a[s * SUB:(s + 1) * SUB, :] for s in range(n)]
    lane = lax.broadcasted_iota(jnp.int32, (SUB, NB), 1)
    sub = lax.broadcasted_iota(jnp.int32, (SUB, NB), 0)
    inv = [jnp.where(lane == sub + s * SUB, 1.0, 0.0).astype(jnp.float32) for s in range(n)]
    for p in range(n):
        for s in range(p, n):
            for c in range(SUB):
                held[p % 2, s, c] = spread(rows[s][:, p * SUB + c:p * SUB + c + 1])
        cols = {s: [held[p % 2, s, c] for c in range(SUB)] for s in range(p, n)}
        for c in range(SUB):
            over = 1.0 / spread(cols[p][c][c:c + 1, :])
            row, inverse = spread(rows[p][c:c + 1, :]), spread(inv[p][c:c + 1, :])
            heads = [spread(cols[p][d][c:c + 1, :]) for d in range(c + 1, SUB)]
            for s in range(p, n):
                m = cols[s][c] * over
                if s == p:
                    m = jnp.where(sub > c, m, 0.0)
                rows[s] = rows[s] - m * row
                inv[s] = inv[s] - m * inverse
                for d, head in zip(range(c + 1, SUB), heads):
                    cols[s][d] = cols[s][d] - m * head
    out = []
    for s in range(n):
        d = jnp.sum(jnp.where(lane == sub + s * SUB, rows[s], 0.0), axis=1, keepdims=True)
        out.append(inv[s] / jnp.sqrt(d))
    return jnp.concatenate(out, axis=0)


def invert(work, top, held):
    size = work.shape[0]
    blocks = size // NB

    def step(b, carry):
        at = pl.multiple_of(b * NB, NB)
        small = block_inverse(work[pl.ds(at, NB), pl.ds(at, NB)], held)
        top[...] = jnp.dot(small, work[pl.ds(at, NB), :], preferred_element_type=jnp.float32, precision=HIGH)
        work[pl.ds(at, NB), :] = top[...]

        def lower(c, carry):
            to = pl.multiple_of(c * NB, NB)
            work[pl.ds(to, NB), :] -= lax.dot_general(
                top[:, pl.ds(to, NB)], top[...], TN, preferred_element_type=jnp.float32, precision=HIGH)
            return carry

        return lax.fori_loop(b + 1, blocks, lower, carry)

    lax.fori_loop(0, blocks, step, 0)


def eye_mask(size):
    return lax.broadcasted_iota(jnp.int32, (size, size), 0) == lax.broadcasted_iota(jnp.int32, (size, size), 1)


def mm(a, b, dims=NN):
    return lax.dot_general(a, b, dims, preferred_element_type=jnp.float32)


def halves(a):
    hi = a.astype(jnp.bfloat16)
    return hi, (a - hi.astype(jnp.float32)).astype(jnp.bfloat16)


def mm2(a, b, dims=NN):
    hi, lo = halves(a)
    return mm(lo, b, dims) + mm(hi, b, dims)


def mm3(a, b, dims=NN):
    hi, lo = halves(a)
    bhi, blo = halves(b)
    return mm(lo, bhi, dims) + mm(hi, blo, dims) + mm(hi, bhi, dims)


def first_kernel(scale, info, s0_ref, r0_ref, i0_ref, work, top, held):
    size = s0_ref.shape[1]
    eye = eye_mask(size)
    work[:, :size] = mm(s0_ref[...], s0_ref[...], TN) * scale + jnp.where(eye, r0_ref[...], 0.0)
    work[:, size:] = jnp.where(eye, 1.0, 0.0)
    invert(work, top, held)
    i0_ref[...] = work[:, size:]


def second_kernel(scale, info, s0_ref, s1_ref, sj_ref, r0_ref, r1_ref, i0_ref, c01_ref, c0j_ref, i1_ref, work, top, held):
    size = s0_ref.shape[1]
    eye = eye_mask(size)
    i0 = i0_ref[...]
    c01 = mm3(i0, mm(s0_ref[...], s1_ref[...], TN) * scale).astype(jnp.bfloat16)
    c01_ref[...] = c01
    r0 = r0_ref[...] * (info[3] == 0).astype(jnp.float32)
    c0j_ref[...] = mm3(i0, mm(s0_ref[...], sj_ref[...], TN) * scale + jnp.where(eye, r0, 0.0)).astype(jnp.bfloat16)
    work[:, :size] = mm(s1_ref[...], s1_ref[...], TN) * scale + jnp.where(eye, r1_ref[...], 0.0) - mm(c01, c01, TN)
    work[:, size:] = jnp.where(eye, 1.0, 0.0)
    invert(work, top, held)
    i1_ref[...] = work[:, size:]


def third_kernel(
    scale, info, s0_ref, s1_ref, sj_ref, r0_ref, r1_ref, i0_ref, i1_ref, c01_ref, c0j_ref, w_ref, p_ref, d_ref
):
    size = s0_ref.shape[1]
    eye = eye_mask(size)
    live = (info[3] > 1).astype(jnp.float32)
    i0, i1, c01, c0j = i0_ref[...], i1_ref[...], c01_ref[...], c0j_ref[...]
    r1 = r1_ref[...]
    w = w_ref[...]
    p0 = mm3(mm(w, s0_ref[...], TN) * scale, i0, NT)
    p_ref[:, :size] = p0.astype(jnp.bfloat16)
    p1 = mm3(mm(w, s1_ref[...], TN) * scale - mm2(p0, c01), i1, NT)
    p_ref[:, size:2 * size] = p1.astype(jnp.bfloat16)
    own = r1 * (info[3] == 1).astype(jnp.float32)
    a1j = mm(s1_ref[...], sj_ref[...], TN) * scale + jnp.where(eye, own, 0.0) - mm(c01, c0j, TN)
    c1j = mm3(i1, a1j).astype(jnp.bfloat16)
    pn = mm(w, sj_ref[...], TN) * scale - mm2(p0, c0j) - mm2(p1, c1j)
    p_ref[:, 2 * size:] = (pn * live).astype(jnp.bfloat16)
    d00 = (i0 * r0_ref[...]).T
    d10 = mm3(-mm2(d00, c01), i1, NT)
    d11 = (i1 * r1).T
    d_ref[:size, :size] = d00
    d_ref[:size, size:2 * size] = d10
    d_ref[:size, 2 * size:] = (mm2(d00, c0j) + mm2(d10, c1j)) * -live
    d_ref[size:, :size] = jnp.zeros((size, size), jnp.float32)
    d_ref[size:, size:2 * size] = d11
    d_ref[size:, 2 * size:] = mm2(d11, c1j) * -live


def chain_call(kernel, info, operands, specs, outs, scratch, flops, name):
    def spec(x, pick, width):
        if pick is None:
            return pl.BlockSpec(x.shape, lambda i, info: (0, 0))
        return pl.BlockSpec((x.shape[0], width), lambda i, info: (0, info[pick]))

    width = outs[0].shape[-1] if name != "third" else outs[0].shape[-1] // 3
    return pl.pallas_call(
        kernel,
        grid_spec=pltpu.PrefetchScalarGridSpec(
            num_scalar_prefetch=1,
            grid=(1,),
            in_specs=[spec(x, p, width) for x, p in zip(operands, specs)],
            out_specs=[pl.BlockSpec(o.shape, lambda i, info: (0, 0)) for o in outs],
            scratch_shapes=scratch,
        ),
        out_shape=outs,
        compiler_params=pltpu.CompilerParams(vmem_limit_bytes=60 * 2**20),
        cost_estimate=pl.CostEstimate(flops=flops, bytes_accessed=8 * 2**20, transcendentals=0),
    )(info, *operands)


def gather_kernel(
    row_n, col_n, tm_n, part, ridge, w, out, ridges, summed, series,
    sum_send, sum_recv, row_send, row_recv, far_send, far_recv, near_send, near_recv, r_send, r_recv,
):
    row, col, tm = lax.axis_index("row"), lax.axis_index("col"), lax.axis_index("tm")
    plane = col_n * tm_n
    me = col * tm_n + tm
    times = part.shape[0]
    share = out.shape[1] // plane
    wide = share // 2

    def member(distance):
        other = lax.rem(me + distance, plane)
        return {"col": other // tm_n, "tm": lax.rem(other, tm_n)}

    def columns(owner, h):
        return pl.ds(pl.multiple_of(owner * share + h * wide, wide), wide)

    barrier = pltpu.get_barrier_semaphore()
    for d in range(1, plane):
        pl.semaphore_signal(barrier, inc=1, device_id=member(d), device_id_type=MESH)
    for d in range(1, row_n):
        pl.semaphore_signal(barrier, inc=1, device_id={"row": lax.rem(row + d, row_n)}, device_id_type=MESH)
    pl.semaphore_wait(barrier, plane + row_n - 2)

    def remote(src, dst, send, recv, to):
        return pltpu.make_async_remote_copy(
            src_ref=src, dst_ref=dst, send_sem=send, recv_sem=recv, device_id=to, device_id_type=MESH)

    def sum_copy(h, d):
        return remote(part.at[:, columns(lax.rem(me + d, plane), h)], summed.at[h, d - 1],
                      sum_send.at[h, d - 1], sum_recv.at[h, d - 1], member(d))

    def row_copy(h, d):
        return remote(series.at[h, pl.ds(0, times)], series.at[h, pl.ds(d * times, times)],
                      row_send.at[h, d - 1], row_recv.at[h, d - 1], {"row": lax.rem(row + d, row_n)})

    steps = [(a, b) for a in range(0, col_n, 2) for b in range(tm_n)]

    def origin(e):
        return lax.rem(col - steps[e][0] + col_n, col_n) * tm_n + lax.rem(tm - steps[e][1] + tm_n, tm_n)

    def far_copy(h, e):
        to = {"col": lax.rem(col + steps[e][0], col_n), "tm": lax.rem(tm + steps[e][1], tm_n)}
        at = columns(me, h)
        return remote(out.at[:, at], out.at[:, at], far_send.at[h, e - 1], far_recv.at[h, e - 1], to)

    def near_copy(h, e):
        at = columns(origin(e), h)
        return remote(out.at[:, at], out.at[:, at], near_send.at[h, e], near_recv.at[h, e],
                      {"col": col + 1 - 2 * lax.rem(col, 2)})

    def ridge_copy(d):
        return remote(ridge, ridges.at[col], r_send.at[d - 1], r_recv.at[d - 1], {"col": lax.rem(col + d, col_n)})

    started = []

    def start(copy):
        copy.start()
        started.append(copy)

    for h in range(2):
        for d in range(1, plane):
            start(sum_copy(h, d))
    for d in range(1, col_n):
        start(ridge_copy(d))
    ridges[col] = ridge[...]
    for h in range(2):
        total = part[:, columns(me, h)].astype(jnp.float32)
        for d in range(1, plane):
            sum_copy(h, d).wait_recv()
            total = total + summed[h, d - 1].astype(jnp.float32)
        series[h, pl.ds(0, times)] = total.astype(jnp.bfloat16)
        for d in range(1, row_n):
            start(row_copy(h, d))
    for h in range(2):
        for d in range(1, row_n):
            row_copy(h, d).wait_recv()
        out[:, columns(me, h)] = mm(w[...], series[h]).astype(jnp.bfloat16)
        for e in range(1, len(steps)):
            start(far_copy(h, e))
        start(near_copy(h, 0))
    for h in range(2):
        for e in range(1, len(steps)):
            far_copy(h, e).wait_recv()
            start(near_copy(h, e))
    for d in range(1, col_n):
        ridge_copy(d).wait_recv()
    for h in range(2):
        for e in range(len(steps)):
            near_copy(h, e).wait_recv()
    for copy in started:
        copy.wait_send()


def gather_slab(part, ridge, w, row_n, col_n, tm_n):
    times, slab = part.shape
    depth = w.shape[0]
    plane = col_n * tm_n
    wide = slab // plane // 2
    far = col_n // 2 * tm_n
    dma = pltpu.SemaphoreType.DMA
    vmem = pl.BlockSpec(memory_space=pltpu.VMEM)
    return pl.pallas_call(
        functools.partial(gather_kernel, row_n, col_n, tm_n),
        out_shape=[jax.ShapeDtypeStruct((depth, slab), jnp.bfloat16),
                   jax.ShapeDtypeStruct((col_n,) + ridge.shape, jnp.float32)],
        in_specs=[vmem] * 3,
        out_specs=[vmem] * 2,
        scratch_shapes=[
            pltpu.VMEM((2, plane - 1, times, wide), jnp.bfloat16),
            pltpu.VMEM((2, depth, wide), jnp.bfloat16),
            dma((2, plane - 1)), dma((2, plane - 1)), dma((2, row_n - 1)), dma((2, row_n - 1)),
            dma((2, far - 1)), dma((2, far - 1)), dma((2, far)), dma((2, far)),
            dma((col_n - 1,)), dma((col_n - 1,)),
        ],
        compiler_params=pltpu.CompilerParams(
            collective_id=1, has_side_effects=True, vmem_limit_bytes=40 * 2**20),
        cost_estimate=pl.CostEstimate(flops=40 * 10**9, bytes_accessed=2**20, transcendentals=0),
        name="gather_slab",
    )(part, ridge, w)


def split_kernel(rows, info, x_ref, *outs):
    for k in range(rows):
        @pl.when(info[0] == k)
        def _():
            for s, o in enumerate(outs):
                o[...] = x_ref[:, (k + s) % rows, :]


def split_blocks(row, x, first, w):
    times, rows, _ = x.shape
    bt = min(64, times)
    return pl.pallas_call(
        functools.partial(split_kernel, rows),
        grid_spec=pltpu.PrefetchScalarGridSpec(
            num_scalar_prefetch=1,
            grid=(times // bt,),
            in_specs=[pl.BlockSpec((bt, rows, w), lambda i, info: (i, 0, first // w))],
            out_specs=[pl.BlockSpec((bt, w), lambda i, info: (i, 0))] * rows,
        ),
        out_shape=[jax.ShapeDtypeStruct((times, w), x.dtype)] * rows,
        cost_estimate=pl.CostEstimate(flops=0, bytes_accessed=4 * times * rows * w * 2, transcendentals=0),
        name="split_blocks",
    )(row, x)


def final_body(chunk_base, info, own_ref, rest_ref, p_ref, d_ref, r_ref, *rest):
    t_ref, f_ref = rest[-2:]
    _, width = t_ref.shape
    times = own_ref.shape[1]
    acc = mm(own_ref[0], p_ref[:times, :], TN) + mm(rest_ref[0], p_ref[times:, :], TN)
    kind = kind_of(info, chunk_base(pl.program_id(0), pl.program_id(1)))

    def put(first, second, last):
        f_ref[0] = first.astype(f_ref.dtype)
        f_ref[1] = second.astype(f_ref.dtype)
        t_ref[...] = last

    @pl.when(kind < 2)
    def _():
        full = acc + d_ref[...]
        put(full[:, :width], full[:, width:2 * width], full[:, 2 * width:])

    @pl.when(kind == 2)
    def _():
        put(acc[:, :width], acc[:, width:2 * width],
            acc[:, 2 * width:] + jnp.where(eye_mask(width), r_ref[...], 0.0))

    @pl.when(kind > 2)
    def _():
        put(acc[:, :width], acc[:, width:2 * width], acc[:, 2 * width:])


def kind_of(info, block):
    at = block - info[4]
    inside = (at >= 0) & (at < info[5])
    kind = jnp.where(at == info[0], 0, jnp.where(at == info[1], 1, jnp.where(at == info[2], 2, 3)))
    return jnp.where(inside, kind, 3)


def final_chunk(info, own, others, weights, d, ridge, prior, chunk, chunks, width):
    cols, times, local = own.shape
    bm = width
    w = local // chunks
    per = w // bm
    rows = cols * local
    rest = others.shape[1]

    def base(c, i):
        return c * (local // bm) + chunk * per + i

    in_specs = [
        pl.BlockSpec((1, times, bm), lambda c, i, info: (c, 0, chunk * per + i)),
        pl.BlockSpec((1, rest, bm), lambda c, i, info: (c, 0, i)),
        pl.BlockSpec(weights.shape, lambda c, i, info: (0, 0)),
        pl.BlockSpec((bm, 3 * width), lambda c, i, info: (jnp.where(kind_of(info, base(c, i)) == 1, 1, 0), 0)),
        pl.BlockSpec((1, width), lambda c, i, info: (0, 0)),
    ]
    operands = [info, own, others, weights, d, ridge]
    aliases = {}
    if prior is not None:
        in_specs += [pl.BlockSpec(memory_space=pl.ANY)] * 2
        aliases = {len(operands): 0, len(operands) + 1: 1}
        operands += list(prior)
    return pl.pallas_call(
        functools.partial(final_body, base),
        grid_spec=pltpu.PrefetchScalarGridSpec(
            num_scalar_prefetch=1,
            grid=(cols, per),
            in_specs=in_specs,
            out_specs=[
                pl.BlockSpec((bm, width), lambda c, i, info: (base(c, i), 0)),
                pl.BlockSpec((2, bm, width), lambda c, i, info: (0, base(c, i), 0)),
            ],
        ),
        out_shape=[
            jax.ShapeDtypeStruct((rows, width), jnp.float32),
            jax.ShapeDtypeStruct((2, rows, width), jnp.bfloat16),
        ],
        input_output_aliases=aliases,
        compiler_params=pltpu.CompilerParams(
            vmem_limit_bytes=48 * 2**20, dimension_semantics=("arbitrary", "arbitrary")
        ),
        cost_estimate=pl.CostEstimate(
            flops=2 * cols * w * (times + rest) * 3 * width, bytes_accessed=cols * w * 6 * 2**10, transcendentals=0),
        name="final",
    )(*operands)


def on_device(samples, whitening, ridge, slab_start, panels):
    times, groups, _, local = samples.shape
    rows = lax.axis_size("row")
    cols = lax.axis_size("col")
    tms = lax.axis_size("tm")
    width = ridge.shape[0]
    slab = width * cols
    kd = local * cols
    depth = whitening.shape[0]
    scale = 1.0 / math.sqrt(depth)
    me_col = lax.axis_index("col")
    me_tm = lax.axis_index("tm")
    me_row = lax.axis_index("row")

    first = slab_start[0] * slab
    group = first // (tms * kd)
    tm_owner = (first % (tms * kd)) // kd
    offset = first % kd

    mine = lax.dynamic_index_in_dim(samples[:, :, 0], group, 1, keepdims=False)
    pieces = []
    for p in range(cols):
        at = offset + p * width
        have = (me_tm == tm_owner) & (me_col == at // local)
        part = lax.dynamic_slice_in_dim(mine, at % local, width, 1)
        pieces.append(jnp.where(have, part, jnp.zeros_like(part)))
    part = jnp.concatenate(pieces, axis=1)
    order = (me_row - jnp.arange(rows)) % rows
    turned = jnp.take(whitening.reshape(depth, rows, times), order, axis=1).reshape(depth, depth)
    sw, ridges = gather_slab(part, jnp.broadcast_to(ridge, (SUB, width)), turned, rows, cols, tms)
    ridges = ridges[:, 0].reshape(1, slab)

    chunks = 4 if local >= 4096 else 2
    w = local // chunks
    flat = samples.reshape(times, groups, local)
    row_info, sw = lax.optimization_barrier((me_row.reshape(1).astype(jnp.int32), sw))
    blocks = [split_blocks(row_info, flat, c * w, w) for c in range(chunks)]
    blocks, sw = lax.optimization_barrier((blocks, sw))
    moved = []
    for c in range(chunks):
        moved.append([
            lax.ppermute(blocks[c][s], "row", [(i, (i + s) % rows) for i in range(rows)]) for s in range(1, rows)
        ])
    own = lax.all_gather(jnp.concatenate([b[0] for b in blocks], axis=1), "col", axis=0)
    others = []
    for m in moved:
        others.append(lax.all_gather(jnp.concatenate(m, axis=0), "col", axis=0))

    q0, q1 = panels[0], panels[1]
    owner = (me_row == group) & (me_tm == tm_owner)
    kind = jnp.where(me_col == q0, 0, jnp.where(me_col == q1, 1, 2))
    info = jnp.stack([
        q0, q1, me_col, kind, offset // width, jnp.where(owner, cols, 0),
    ]).astype(jnp.int32)
    square = jax.ShapeDtypeStruct((width, width), jnp.float32)
    coarse = jax.ShapeDtypeStruct((width, width), jnp.bfloat16)
    scratch = [pltpu.VMEM((width, 2 * width), jnp.float32), pltpu.VMEM((NB, 2 * width), jnp.float32),
               pltpu.VMEM((2, NB // SUB, SUB, SUB, NB), jnp.float32)]
    i0, = chain_call(
        functools.partial(first_kernel, scale), info, [sw, ridges], [0, 0], [square], scratch, 20 * 10**9, "first")
    c01, c0j, i1 = chain_call(
        functools.partial(second_kernel, scale), info, [sw, sw, sw, ridges, ridges, i0], [0, 1, 2, 0, 1, None],
        [coarse, coarse, square], scratch, 24 * 10**9, "second")
    weights, d = chain_call(
        functools.partial(third_kernel, scale), info,
        [sw, sw, sw, ridges, ridges, i0, i1, c01, c0j, turned], [0, 1, 2, 0, 1, None, None, None, None, None],
        [jax.ShapeDtypeStruct((depth, 3 * width), jnp.bfloat16), jax.ShapeDtypeStruct((2 * width, 3 * width), jnp.float32)],
        [], 15 * 10**9, "third")
    own_ridge = ridge.reshape(1, width) * (kind == 2).astype(jnp.float32)

    prior = None
    for c in range(chunks):
        prior = final_chunk(info, own, others[c], weights, d, own_ridge, prior, c, chunks, width)
    return tuple(prior)


def solution(mesh):
    in_specs = (P("row", None, "tm", "col"), P(), P("col"), P(), P())
    out_specs = (P(("row", "tm"), "col"), P(None, ("row", "tm"), None))
    return jax.shard_map(on_device, mesh=mesh, in_specs=in_specs, out_specs=out_specs, check_vma=False)
```

```python
import functools
import math
import jax
import jax.numpy as jnp
from jax import lax
from jax.experimental import pallas as pl
from jax.experimental.pallas import tpu as pltpu
from jax.sharding import PartitionSpec as P

NB = 128
SUB = 8
HIGH = lax.Precision.HIGHEST
MESH = pl.DeviceIdType.MESH
NN = (((1,), (0,)), ((), ()))
NT = (((1,), (1,)), ((), ()))
TN = (((0,), (0,)), ((), ()))


def spread(x):
    return jnp.broadcast_to(x, (SUB, NB))


def block_inverse(a, held):
    n = NB // SUB
    rows = [a[s * SUB:(s + 1) * SUB, :] for s in range(n)]
    lane = lax.broadcasted_iota(jnp.int32, (SUB, NB), 1)
    sub = lax.broadcasted_iota(jnp.int32, (SUB, NB), 0)
    inv = [jnp.where(lane == sub + s * SUB, 1.0, 0.0).astype(jnp.float32) for s in range(n)]
    for p in range(n):
        for s in range(p, n):
            for c in range(SUB):
                held[p % 2, s, c] = spread(rows[s][:, p * SUB + c:p * SUB + c + 1])
        cols = {s: [held[p % 2, s, c] for c in range(SUB)] for s in range(p, n)}
        for c in range(SUB):
            over = 1.0 / spread(cols[p][c][c:c + 1, :])
            row, inverse = spread(rows[p][c:c + 1, :]), spread(inv[p][c:c + 1, :])
            heads = [spread(cols[p][d][c:c + 1, :]) for d in range(c + 1, SUB)]
            for s in range(p, n):
                m = cols[s][c] * over
                if s == p:
                    m = jnp.where(sub > c, m, 0.0)
                rows[s] = rows[s] - m * row
                inv[s] = inv[s] - m * inverse
                for d, head in zip(range(c + 1, SUB), heads):
                    cols[s][d] = cols[s][d] - m * head
    out = []
    for s in range(n):
        d = jnp.sum(jnp.where(lane == sub + s * SUB, rows[s], 0.0), axis=1, keepdims=True)
        out.append(inv[s] / jnp.sqrt(d))
    return jnp.concatenate(out, axis=0)


def invert(work, top, held):
    size = work.shape[0]
    blocks = size // NB

    def step(b, carry):
        at = pl.multiple_of(b * NB, NB)
        small = block_inverse(work[pl.ds(at, NB), pl.ds(at, NB)], held)
        top[...] = jnp.dot(small, work[pl.ds(at, NB), :], preferred_element_type=jnp.float32, precision=HIGH)
        work[pl.ds(at, NB), :] = top[...]

        def lower(c, carry):
            to = pl.multiple_of(c * NB, NB)
            work[pl.ds(to, NB), :] -= lax.dot_general(
                top[:, pl.ds(to, NB)], top[...], TN, preferred_element_type=jnp.float32, precision=HIGH)
            return carry

        return lax.fori_loop(b + 1, blocks, lower, carry)

    lax.fori_loop(0, blocks, step, 0)


def eye_mask(size):
    return lax.broadcasted_iota(jnp.int32, (size, size), 0) == lax.broadcasted_iota(jnp.int32, (size, size), 1)


def mm(a, b, dims=NN):
    return lax.dot_general(a, b, dims, preferred_element_type=jnp.float32)


def halves(a):
    hi = a.astype(jnp.bfloat16)
    return hi, (a - hi.astype(jnp.float32)).astype(jnp.bfloat16)


def mm2(a, b, dims=NN):
    hi, lo = halves(a)
    return mm(lo, b, dims) + mm(hi, b, dims)


def mm3(a, b, dims=NN):
    hi, lo = halves(a)
    bhi, blo = halves(b)
    return mm(lo, bhi, dims) + mm(hi, blo, dims) + mm(hi, bhi, dims)


def first_kernel(scale, info, s0_ref, r0_ref, i0_ref, work, top, held):
    size = s0_ref.shape[1]
    eye = eye_mask(size)
    work[:, :size] = mm(s0_ref[...], s0_ref[...], TN) * scale + jnp.where(eye, r0_ref[...], 0.0)
    work[:, size:] = jnp.where(eye, 1.0, 0.0)
    invert(work, top, held)
    i0_ref[...] = work[:, size:]


def second_kernel(scale, info, s0_ref, s1_ref, sj_ref, r0_ref, r1_ref, i0_ref, c01_ref, c0j_ref, i1_ref, work, top, held):
    size = s0_ref.shape[1]
    eye = eye_mask(size)
    i0 = i0_ref[...]
    c01 = mm3(i0, mm(s0_ref[...], s1_ref[...], TN) * scale).astype(jnp.bfloat16)
    c01_ref[...] = c01
    r0 = r0_ref[...] * (info[3] == 0).astype(jnp.float32)
    c0j_ref[...] = mm3(i0, mm(s0_ref[...], sj_ref[...], TN) * scale + jnp.where(eye, r0, 0.0)).astype(jnp.bfloat16)
    work[:, :size] = mm(s1_ref[...], s1_ref[...], TN) * scale + jnp.where(eye, r1_ref[...], 0.0) - mm(c01, c01, TN)
    work[:, size:] = jnp.where(eye, 1.0, 0.0)
    invert(work, top, held)
    i1_ref[...] = work[:, size:]


def third_kernel(
    scale, rows, info, s0_ref, s1_ref, sj_ref, r0_ref, r1_ref, i0_ref, i1_ref, c01_ref, c0j_ref, w_ref, p_ref, d_ref
):
    size = s0_ref.shape[1]
    eye = eye_mask(size)
    live = (info[3] > 1).astype(jnp.float32)
    i0, i1, c01, c0j = i0_ref[...], i1_ref[...], c01_ref[...], c0j_ref[...]
    r1 = r1_ref[...]
    w = w_ref[...]
    times = w.shape[0] // rows

    def put(value, side):
        for t in range(rows):
            to = pl.multiple_of(lax.rem(info[6] - t + rows, rows) * times, times)
            p_ref[pl.ds(to, times), side * size:(side + 1) * size] = value[t * times:(t + 1) * times].astype(jnp.bfloat16)

    p0 = mm3(mm(w, s0_ref[...], TN) * scale, i0, NT)
    put(p0, 0)
    p1 = mm3(mm(w, s1_ref[...], TN) * scale - mm2(p0, c01), i1, NT)
    put(p1, 1)
    own = r1 * (info[3] == 1).astype(jnp.float32)
    a1j = mm(s1_ref[...], sj_ref[...], TN) * scale + jnp.where(eye, own, 0.0) - mm(c01, c0j, TN)
    c1j = mm3(i1, a1j).astype(jnp.bfloat16)
    pn = mm(w, sj_ref[...], TN) * scale - mm2(p0, c0j) - mm2(p1, c1j)
    put(pn * live, 2)
    d00 = (i0 * r0_ref[...]).T
    d10 = mm3(-mm2(d00, c01), i1, NT)
    d11 = (i1 * r1).T
    d_ref[:size, :size] = d00
    d_ref[:size, size:2 * size] = d10
    d_ref[:size, 2 * size:] = (mm2(d00, c0j) + mm2(d10, c1j)) * -live
    d_ref[size:, :size] = jnp.zeros((size, size), jnp.float32)
    d_ref[size:, size:2 * size] = d11
    d_ref[size:, 2 * size:] = mm2(d11, c1j) * -live


def chain_call(kernel, info, operands, specs, outs, scratch, flops, name):
    def spec(x, pick, width):
        if pick is None:
            return pl.BlockSpec(x.shape, lambda i, info: (0, 0))
        return pl.BlockSpec((x.shape[0], width), lambda i, info: (0, info[pick]))

    width = outs[0].shape[-1] if name != "third" else outs[0].shape[-1] // 3
    return pl.pallas_call(
        kernel,
        grid_spec=pltpu.PrefetchScalarGridSpec(
            num_scalar_prefetch=1,
            grid=(1,),
            in_specs=[spec(x, p, width) for x, p in zip(operands, specs)],
            out_specs=[pl.BlockSpec(o.shape, lambda i, info: (0, 0)) for o in outs],
            scratch_shapes=scratch,
        ),
        out_shape=outs,
        compiler_params=pltpu.CompilerParams(vmem_limit_bytes=60 * 2**20),
        cost_estimate=pl.CostEstimate(flops=flops, bytes_accessed=8 * 2**20, transcendentals=0),
    )(info, *operands)


def gather_kernel(
    row_n, col_n, tm_n, part, ridge, w, out, ridges, summed, series,
    sum_send, sum_recv, row_send, row_recv, far_send, far_recv, near_send, near_recv, r_send, r_recv,
):
    row, col, tm = lax.axis_index("row"), lax.axis_index("col"), lax.axis_index("tm")
    plane = col_n * tm_n
    me = col * tm_n + tm
    times = part.shape[0]
    here = pl.ds(pl.multiple_of(row * times, times), times)
    share = out.shape[1] // plane
    wide = share // 2

    def member(distance):
        other = lax.rem(me + distance, plane)
        return {"col": other // tm_n, "tm": lax.rem(other, tm_n)}

    def columns(owner, h):
        return pl.ds(pl.multiple_of(owner * share + h * wide, wide), wide)

    barrier = pltpu.get_barrier_semaphore()
    for d in range(1, plane):
        pl.semaphore_signal(barrier, inc=1, device_id=member(d), device_id_type=MESH)
    for d in range(1, row_n):
        pl.semaphore_signal(barrier, inc=1, device_id={"row": lax.rem(row + d, row_n)}, device_id_type=MESH)
    pl.semaphore_wait(barrier, plane + row_n - 2)

    def remote(src, dst, send, recv, to):
        return pltpu.make_async_remote_copy(
            src_ref=src, dst_ref=dst, send_sem=send, recv_sem=recv, device_id=to, device_id_type=MESH)

    def sum_copy(h, d):
        return remote(part.at[:, columns(lax.rem(me + d, plane), h)], summed.at[h, d - 1],
                      sum_send.at[h, d - 1], sum_recv.at[h, d - 1], member(d))

    def row_copy(h, d):
        return remote(series.at[h, here], series.at[h, here],
                      row_send.at[h, d - 1], row_recv.at[h, d - 1], {"row": lax.rem(row + d, row_n)})

    steps = [(a, b) for a in range(0, col_n, 2) for b in range(tm_n)]

    def origin(e):
        return lax.rem(col - steps[e][0] + col_n, col_n) * tm_n + lax.rem(tm - steps[e][1] + tm_n, tm_n)

    def far_copy(h, e):
        to = {"col": lax.rem(col + steps[e][0], col_n), "tm": lax.rem(tm + steps[e][1], tm_n)}
        at = columns(me, h)
        return remote(out.at[:, at], out.at[:, at], far_send.at[h, e - 1], far_recv.at[h, e - 1], to)

    def near_copy(h, e):
        at = columns(origin(e), h)
        return remote(out.at[:, at], out.at[:, at], near_send.at[h, e], near_recv.at[h, e],
                      {"col": col + 1 - 2 * lax.rem(col, 2)})

    def ridge_copy(d):
        return remote(ridge, ridges.at[col], r_send.at[d - 1], r_recv.at[d - 1], {"col": lax.rem(col + d, col_n)})

    started = []

    def start(copy):
        copy.start()
        started.append(copy)

    for h in range(2):
        for d in range(1, plane):
            start(sum_copy(h, d))
    for d in range(1, col_n):
        start(ridge_copy(d))
    ridges[col] = ridge[...]
    for h in range(2):
        total = part[:, columns(me, h)].astype(jnp.float32)
        for d in range(1, plane):
            sum_copy(h, d).wait_recv()
            total = total + summed[h, d - 1].astype(jnp.float32)
        series[h, here] = total.astype(jnp.bfloat16)
        for d in range(1, row_n):
            start(row_copy(h, d))
    for h in range(2):
        for d in range(1, row_n):
            row_copy(h, d).wait_recv()
        out[:, columns(me, h)] = mm(w[...], series[h]).astype(jnp.bfloat16)
        for e in range(1, len(steps)):
            start(far_copy(h, e))
        start(near_copy(h, 0))
    for h in range(2):
        for e in range(1, len(steps)):
            far_copy(h, e).wait_recv()
            start(near_copy(h, e))
    for d in range(1, col_n):
        ridge_copy(d).wait_recv()
    for h in range(2):
        for e in range(len(steps)):
            near_copy(h, e).wait_recv()
    for copy in started:
        copy.wait_send()


def gather_slab(part, ridge, w, row_n, col_n, tm_n):
    times, slab = part.shape
    depth = w.shape[0]
    plane = col_n * tm_n
    wide = slab // plane // 2
    far = col_n // 2 * tm_n
    dma = pltpu.SemaphoreType.DMA
    vmem = pl.BlockSpec(memory_space=pltpu.VMEM)
    return pl.pallas_call(
        functools.partial(gather_kernel, row_n, col_n, tm_n),
        out_shape=[jax.ShapeDtypeStruct((depth, slab), jnp.bfloat16),
                   jax.ShapeDtypeStruct((col_n,) + ridge.shape, jnp.float32)],
        in_specs=[vmem] * 3,
        out_specs=[vmem] * 2,
        scratch_shapes=[
            pltpu.VMEM((2, plane - 1, times, wide), jnp.bfloat16),
            pltpu.VMEM((2, depth, wide), jnp.bfloat16),
            dma((2, plane - 1)), dma((2, plane - 1)), dma((2, row_n - 1)), dma((2, row_n - 1)),
            dma((2, far - 1)), dma((2, far - 1)), dma((2, far)), dma((2, far)),
            dma((col_n - 1,)), dma((col_n - 1,)),
        ],
        compiler_params=pltpu.CompilerParams(
            collective_id=1, has_side_effects=True, vmem_limit_bytes=40 * 2**20),
        cost_estimate=pl.CostEstimate(flops=40 * 10**9, bytes_accessed=2**20, transcendentals=0),
        name="gather_slab",
    )(part, ridge, w)


def split_kernel(rows, info, x_ref, *outs):
    for k in range(rows):
        @pl.when(info[0] == k)
        def _():
            for s, o in enumerate(outs):
                o[...] = x_ref[:, (k + s + 1) % rows, :]


def split_blocks(row, x, first, w):
    times, rows, _ = x.shape
    bt = min(64, times)
    return pl.pallas_call(
        functools.partial(split_kernel, rows),
        grid_spec=pltpu.PrefetchScalarGridSpec(
            num_scalar_prefetch=1,
            grid=(times // bt,),
            in_specs=[pl.BlockSpec((bt, rows, w), lambda i, info: (i, 0, first // w))],
            out_specs=[pl.BlockSpec((bt, w), lambda i, info: (i, 0))] * (rows - 1),
        ),
        out_shape=[jax.ShapeDtypeStruct((times, w), x.dtype)] * (rows - 1),
        cost_estimate=pl.CostEstimate(flops=0, bytes_accessed=4 * times * rows * w * 2, transcendentals=0),
        name="split_blocks",
    )(row, x)


def pick_kernel(rows, info, x_ref, o_ref):
    keep = info[1 + pl.program_id(0)] > 0
    for k in range(rows):
        @pl.when(keep & (info[0] == k))
        def _():
            o_ref[...] = x_ref[:, k, :]

    @pl.when(jnp.logical_not(keep))
    def _():
        o_ref[...] = jnp.zeros_like(o_ref)


def pick_blocks(which, keep, at, x, wide):
    times, rows, _ = x.shape
    n = at.shape[0]
    info = jnp.concatenate([which.reshape(1), keep, at]).astype(jnp.int32)
    return pl.pallas_call(
        functools.partial(pick_kernel, rows),
        grid_spec=pltpu.PrefetchScalarGridSpec(
            num_scalar_prefetch=1,
            grid=(n,),
            in_specs=[pl.BlockSpec((times, rows, wide), lambda p, info: (0, 0, info[1 + n + p]))],
            out_specs=pl.BlockSpec((times, wide), lambda p, info: (0, p)),
        ),
        out_shape=jax.ShapeDtypeStruct((times, n * wide), x.dtype),
        cost_estimate=pl.CostEstimate(flops=0, bytes_accessed=2 * times * rows * n * wide * 2, transcendentals=0),
        name="pick_blocks",
    )(info, x)


def final_body(chunk_base, info, own_ref, rest_ref, p_ref, d_ref, r_ref, *rest):
    t_ref, f_ref = rest[-2:]
    _, width = t_ref.shape
    times = own_ref.shape[1]
    acc = mm(own_ref[0], p_ref[:times, :], TN) + mm(rest_ref[0], p_ref[times:, :], TN)
    kind = kind_of(info, chunk_base(pl.program_id(0), pl.program_id(1)))

    def put(first, second, last):
        f_ref[0] = first.astype(f_ref.dtype)
        f_ref[1] = second.astype(f_ref.dtype)
        t_ref[...] = last

    @pl.when(kind < 2)
    def _():
        full = acc + d_ref[...]
        put(full[:, :width], full[:, width:2 * width], full[:, 2 * width:])

    @pl.when(kind == 2)
    def _():
        put(acc[:, :width], acc[:, width:2 * width],
            acc[:, 2 * width:] + jnp.where(eye_mask(width), r_ref[...], 0.0))

    @pl.when(kind > 2)
    def _():
        put(acc[:, :width], acc[:, width:2 * width], acc[:, 2 * width:])


def kind_of(info, block):
    at = block - info[4]
    inside = (at >= 0) & (at < info[5])
    kind = jnp.where(at == info[0], 0, jnp.where(at == info[1], 1, jnp.where(at == info[2], 2, 3)))
    return jnp.where(inside, kind, 3)


def final_chunk(info, own, others, weights, d, ridge, prior, start, width):
    cols, times, local = own.shape
    bm = width
    w = others.shape[2]
    per = w // bm
    rows = cols * local
    rest = others.shape[1]

    def base(c, i):
        return c * (local // bm) + start // bm + i

    in_specs = [
        pl.BlockSpec((1, times, bm), lambda c, i, info: (c, 0, start // bm + i)),
        pl.BlockSpec((1, rest, bm), lambda c, i, info: (c, 0, i)),
        pl.BlockSpec(weights.shape, lambda c, i, info: (0, 0)),
        pl.BlockSpec((bm, 3 * width), lambda c, i, info: (jnp.where(kind_of(info, base(c, i)) == 1, 1, 0), 0)),
        pl.BlockSpec((1, width), lambda c, i, info: (0, 0)),
    ]
    operands = [info, own, others, weights, d, ridge]
    aliases = {}
    if prior is not None:
        in_specs += [pl.BlockSpec(memory_space=pl.ANY)] * 2
        aliases = {len(operands): 0, len(operands) + 1: 1}
        operands += list(prior)
    return pl.pallas_call(
        functools.partial(final_body, base),
        grid_spec=pltpu.PrefetchScalarGridSpec(
            num_scalar_prefetch=1,
            grid=(cols, per),
            in_specs=in_specs,
            out_specs=[
                pl.BlockSpec((bm, width), lambda c, i, info: (base(c, i), 0)),
                pl.BlockSpec((2, bm, width), lambda c, i, info: (0, base(c, i), 0)),
            ],
        ),
        out_shape=[
            jax.ShapeDtypeStruct((rows, width), jnp.float32),
            jax.ShapeDtypeStruct((2, rows, width), jnp.bfloat16),
        ],
        input_output_aliases=aliases,
        compiler_params=pltpu.CompilerParams(
            vmem_limit_bytes=48 * 2**20, dimension_semantics=("arbitrary", "arbitrary")
        ),
        cost_estimate=pl.CostEstimate(
            flops=2 * cols * w * (times + rest) * 3 * width, bytes_accessed=cols * w * 6 * 2**10, transcendentals=0),
        name="final",
    )(*operands)


def on_device(samples, whitening, ridge, slab_start, panels):
    times, groups, _, local = samples.shape
    rows = lax.axis_size("row")
    cols = lax.axis_size("col")
    tms = lax.axis_size("tm")
    width = ridge.shape[0]
    slab = width * cols
    kd = local * cols
    depth = whitening.shape[0]
    scale = 1.0 / math.sqrt(depth)
    me_col = lax.axis_index("col")
    me_tm = lax.axis_index("tm")
    me_row = lax.axis_index("row")

    first = slab_start[0] * slab
    group = first // (tms * kd)
    tm_owner = (first % (tms * kd)) // kd
    offset = first % kd

    flat = samples.reshape(times, groups, local)
    sizes = [local // 4] * 3 + [local // 8] * 2 if local >= 8 * width else [width] * (local // width)
    starts = [sum(sizes[:c]) for c in range(len(sizes))]
    row_info = me_row.reshape(1).astype(jnp.int32)
    split = lambda row, c: split_blocks(row, flat, starts[c], sizes[c])
    head = split(row_info, 0)
    count = local // width
    own = pick_blocks(me_row, jnp.ones((count,), jnp.int32), jnp.arange(count), flat, width)
    at = offset + jnp.arange(cols) * width
    have = (me_tm == tm_owner) & (me_col == at // local)
    part = pick_blocks(group, have, at % local // width, flat, width)
    part, head, own = lax.optimization_barrier((part, head, own))
    own = lax.all_gather(own, "col", axis=0)
    sw, ridges = gather_slab(part, jnp.broadcast_to(ridge, (SUB, width)), whitening, rows, cols, tms)
    ridges = ridges[:, 0].reshape(1, slab)

    row_info, sw = lax.optimization_barrier((row_info, sw))
    blocks = [split(row_info, c) for c in range(1, len(sizes))]
    blocks, sw = lax.optimization_barrier((blocks, sw))
    others = []
    for block in [head] + blocks:
        moved = [lax.ppermute(block[s - 1], "row", [(i, (i + s) % rows) for i in range(rows)]) for s in range(1, rows)]
        others.append(lax.all_gather(jnp.concatenate(moved, axis=0), "col", axis=0))

    q0, q1 = panels[0], panels[1]
    owner = (me_row == group) & (me_tm == tm_owner)
    kind = jnp.where(me_col == q0, 0, jnp.where(me_col == q1, 1, 2))
    info = jnp.stack([
        q0, q1, me_col, kind, offset // width, jnp.where(owner, cols, 0), me_row,
    ]).astype(jnp.int32)
    square = jax.ShapeDtypeStruct((width, width), jnp.float32)
    coarse = jax.ShapeDtypeStruct((width, width), jnp.bfloat16)
    scratch = [pltpu.VMEM((width, 2 * width), jnp.float32), pltpu.VMEM((NB, 2 * width), jnp.float32),
               pltpu.VMEM((2, NB // SUB, SUB, SUB, NB), jnp.float32)]
    i0, = chain_call(
        functools.partial(first_kernel, scale), info, [sw, ridges], [0, 0], [square], scratch, 20 * 10**9, "first")
    c01, c0j, i1 = chain_call(
        functools.partial(second_kernel, scale), info, [sw, sw, sw, ridges, ridges, i0], [0, 1, 2, 0, 1, None],
        [coarse, coarse, square], scratch, 24 * 10**9, "second")
    weights, d = chain_call(
        functools.partial(third_kernel, scale, rows), info,
        [sw, sw, sw, ridges, ridges, i0, i1, c01, c0j, whitening], [0, 1, 2, 0, 1, None, None, None, None, None],
        [jax.ShapeDtypeStruct((depth, 3 * width), jnp.bfloat16), jax.ShapeDtypeStruct((2 * width, 3 * width), jnp.float32)],
        [], 15 * 10**9, "third")
    own_ridge = ridge.reshape(1, width) * (kind == 2).astype(jnp.float32)

    prior = None
    for c, start in enumerate(starts):
        prior = final_chunk(info, own, others[c], weights, d, own_ridge, prior, start, width)
    return tuple(prior)


def solution(mesh):
    in_specs = (P("row", None, "tm", "col"), P(), P("col"), P(), P())
    out_specs = (P(("row", "tm"), "col"), P(None, ("row", "tm"), None))
    return jax.shard_map(on_device, mesh=mesh, in_specs=in_specs, out_specs=out_specs, check_vma=False)
```

```python
import functools
import math
import jax
import jax.numpy as jnp
from jax import lax
from jax.experimental import pallas as pl
from jax.experimental.pallas import tpu as pltpu
from jax.sharding import PartitionSpec as P

NB = 128
SUB = 8
HIGH = lax.Precision.HIGHEST
MESH = pl.DeviceIdType.MESH
NN = (((1,), (0,)), ((), ()))
NT = (((1,), (1,)), ((), ()))
TN = (((0,), (0,)), ((), ()))


def spread(x):
    return jnp.broadcast_to(x, (SUB, NB))


def block_inverse(a, held):
    n = NB // SUB
    rows = [a[s * SUB:(s + 1) * SUB, :] for s in range(n)]
    lane = lax.broadcasted_iota(jnp.int32, (SUB, NB), 1)
    sub = lax.broadcasted_iota(jnp.int32, (SUB, NB), 0)
    inv = [jnp.where(lane == sub + s * SUB, 1.0, 0.0).astype(jnp.float32) for s in range(n)]
    for p in range(n):
        for s in range(p, n):
            for c in range(SUB):
                held[p % 2, s, c] = spread(rows[s][:, p * SUB + c:p * SUB + c + 1])
        cols = {s: [held[p % 2, s, c] for c in range(SUB)] for s in range(p, n)}
        for c in range(SUB):
            over = 1.0 / spread(cols[p][c][c:c + 1, :])
            row, inverse = spread(rows[p][c:c + 1, :]), spread(inv[p][c:c + 1, :])
            heads = [spread(cols[p][d][c:c + 1, :]) for d in range(c + 1, SUB)]
            for s in range(p, n):
                m = cols[s][c] * over
                if s == p:
                    m = jnp.where(sub > c, m, 0.0)
                rows[s] = rows[s] - m * row
                inv[s] = inv[s] - m * inverse
                for d, head in zip(range(c + 1, SUB), heads):
                    cols[s][d] = cols[s][d] - m * head
    out = []
    for s in range(n):
        d = jnp.sum(jnp.where(lane == sub + s * SUB, rows[s], 0.0), axis=1, keepdims=True)
        out.append(inv[s] / jnp.sqrt(d))
    return jnp.concatenate(out, axis=0)


def invert(work, top, held):
    size = work.shape[0]
    blocks = size // NB

    def step(b, carry):
        at = pl.multiple_of(b * NB, NB)
        small = block_inverse(work[pl.ds(at, NB), pl.ds(at, NB)], held)
        top[...] = jnp.dot(small, work[pl.ds(at, NB), :], preferred_element_type=jnp.float32, precision=HIGH)
        work[pl.ds(at, NB), :] = top[...]

        def lower(c, carry):
            to = pl.multiple_of(c * NB, NB)
            work[pl.ds(to, NB), :] -= lax.dot_general(
                top[:, pl.ds(to, NB)], top[...], TN, preferred_element_type=jnp.float32, precision=HIGH)
            return carry

        return lax.fori_loop(b + 1, blocks, lower, carry)

    lax.fori_loop(0, blocks, step, 0)


def eye_mask(size):
    return lax.broadcasted_iota(jnp.int32, (size, size), 0) == lax.broadcasted_iota(jnp.int32, (size, size), 1)


def mm(a, b, dims=NN):
    return lax.dot_general(a, b, dims, preferred_element_type=jnp.float32)


def halves(a):
    hi = a.astype(jnp.bfloat16)
    return hi, (a - hi.astype(jnp.float32)).astype(jnp.bfloat16)


def mm2(a, b, dims=NN):
    hi, lo = halves(a)
    return mm(lo, b, dims) + mm(hi, b, dims)


def mm3(a, b, dims=NN):
    hi, lo = halves(a)
    bhi, blo = halves(b)
    return mm(lo, bhi, dims) + mm(hi, blo, dims) + mm(hi, bhi, dims)


def first_kernel(scale, info, s0_ref, r0_ref, i0_ref, work, top, held):
    size = s0_ref.shape[1]
    eye = eye_mask(size)
    work[:, :size] = mm(s0_ref[...], s0_ref[...], TN) * scale + jnp.where(eye, r0_ref[...], 0.0)
    work[:, size:] = jnp.where(eye, 1.0, 0.0)
    invert(work, top, held)
    i0_ref[...] = work[:, size:]


def second_kernel(scale, info, s0_ref, s1_ref, sj_ref, r0_ref, r1_ref, i0_ref, c01_ref, c0j_ref, i1_ref, work, top, held):
    size = s0_ref.shape[1]
    eye = eye_mask(size)
    i0 = i0_ref[...]
    c01 = mm3(i0, mm(s0_ref[...], s1_ref[...], TN) * scale).astype(jnp.bfloat16)
    c01_ref[...] = c01
    r0 = r0_ref[...] * (info[3] == 0).astype(jnp.float32)
    c0j_ref[...] = mm3(i0, mm(s0_ref[...], sj_ref[...], TN) * scale + jnp.where(eye, r0, 0.0)).astype(jnp.bfloat16)
    work[:, :size] = mm(s1_ref[...], s1_ref[...], TN) * scale + jnp.where(eye, r1_ref[...], 0.0) - mm(c01, c01, TN)
    work[:, size:] = jnp.where(eye, 1.0, 0.0)
    invert(work, top, held)
    i1_ref[...] = work[:, size:]


def third_kernel(
    scale, rows, info, s0_ref, s1_ref, sj_ref, r0_ref, r1_ref, i0_ref, i1_ref, c01_ref, c0j_ref, w_ref, p_ref, d_ref
):
    size = s0_ref.shape[1]
    eye = eye_mask(size)
    live = (info[3] > 1).astype(jnp.float32)
    i0, i1, c01, c0j = i0_ref[...], i1_ref[...], c01_ref[...], c0j_ref[...]
    r1 = r1_ref[...]
    w = w_ref[...]
    times = w.shape[0] // rows

    def put(value, side):
        for t in range(rows):
            to = pl.multiple_of(lax.rem(info[6] - t + rows, rows) * times, times)
            p_ref[pl.ds(to, times), side * size:(side + 1) * size] = value[t * times:(t + 1) * times].astype(jnp.bfloat16)

    p0 = mm3(mm(w, s0_ref[...], TN) * scale, i0, NT)
    put(p0, 0)
    p1 = mm3(mm(w, s1_ref[...], TN) * scale - mm2(p0, c01), i1, NT)
    put(p1, 1)
    own = r1 * (info[3] == 1).astype(jnp.float32)
    a1j = mm(s1_ref[...], sj_ref[...], TN) * scale + jnp.where(eye, own, 0.0) - mm(c01, c0j, TN)
    c1j = mm3(i1, a1j).astype(jnp.bfloat16)
    pn = mm(w, sj_ref[...], TN) * scale - mm2(p0, c0j) - mm2(p1, c1j)
    put(pn * live, 2)
    d00 = (i0 * r0_ref[...]).T
    d10 = mm3(-mm2(d00, c01), i1, NT)
    d11 = (i1 * r1).T
    d_ref[:size, :size] = d00
    d_ref[:size, size:2 * size] = d10
    d_ref[:size, 2 * size:] = (mm2(d00, c0j) + mm2(d10, c1j)) * -live
    d_ref[size:, :size] = jnp.zeros((size, size), jnp.float32)
    d_ref[size:, size:2 * size] = d11
    d_ref[size:, 2 * size:] = mm2(d11, c1j) * -live


def chain_call(kernel, info, operands, specs, outs, scratch, flops, name):
    def spec(x, pick, width):
        if pick is None:
            return pl.BlockSpec(x.shape, lambda i, info: (0, 0))
        return pl.BlockSpec((x.shape[0], width), lambda i, info: (0, info[pick]))

    width = outs[0].shape[-1] if name != "third" else outs[0].shape[-1] // 3
    return pl.pallas_call(
        kernel,
        grid_spec=pltpu.PrefetchScalarGridSpec(
            num_scalar_prefetch=1,
            grid=(1,),
            in_specs=[spec(x, p, width) for x, p in zip(operands, specs)],
            out_specs=[pl.BlockSpec(o.shape, lambda i, info: (0, 0)) for o in outs],
            scratch_shapes=scratch,
        ),
        out_shape=outs,
        compiler_params=pltpu.CompilerParams(vmem_limit_bytes=60 * 2**20),
        cost_estimate=pl.CostEstimate(flops=flops, bytes_accessed=8 * 2**20, transcendentals=0),
    )(info, *operands)


def gather_kernel(row_n, col_n, tm_n, starts, sizes, part, ridge, w, flat, out, ridges, own, head, *rest):
    count = len(sizes)
    pieces = [rest[c * (row_n - 1):(c + 1) * (row_n - 1)] for c in range(count)]
    (summed, series, source, sorted_, sum_send, sum_recv, row_send, row_recv, far_send, far_recv, near_send, near_recv,
     r_send, r_recv, in_sem, out_sem, head_send, head_recv) = rest[count * (row_n - 1):]
    row, col, tm = lax.axis_index("row"), lax.axis_index("col"), lax.axis_index("tm")
    plane = col_n * tm_n
    me = col * tm_n + tm
    times = part.shape[0]
    here = pl.ds(pl.multiple_of(row * times, times), times)
    share = out.shape[1] // plane
    wide = share // 2

    def member(distance):
        other = lax.rem(me + distance, plane)
        return {"col": other // tm_n, "tm": lax.rem(other, tm_n)}

    def columns(owner, h):
        return pl.ds(pl.multiple_of(owner * share + h * wide, wide), wide)

    barrier = pltpu.get_barrier_semaphore()
    for d in range(1, plane):
        pl.semaphore_signal(barrier, inc=1, device_id=member(d), device_id_type=MESH)
    for d in range(1, row_n):
        pl.semaphore_signal(barrier, inc=1, device_id={"row": lax.rem(row + d, row_n)}, device_id_type=MESH)
    pl.semaphore_wait(barrier, plane + row_n - 2)

    def remote(src, dst, send, recv, to):
        return pltpu.make_async_remote_copy(
            src_ref=src, dst_ref=dst, send_sem=send, recv_sem=recv, device_id=to, device_id_type=MESH)

    def sum_copy(h, d):
        return remote(part.at[:, columns(lax.rem(me + d, plane), h)], summed.at[h, d - 1],
                      sum_send.at[h, d - 1], sum_recv.at[h, d - 1], member(d))

    def row_copy(h, d):
        return remote(series.at[h, here], series.at[h, here],
                      row_send.at[h, d - 1], row_recv.at[h, d - 1], {"row": lax.rem(row + d, row_n)})

    steps = [(a, b) for a in range(0, col_n, 2) for b in range(tm_n)]

    def origin(e):
        return lax.rem(col - steps[e][0] + col_n, col_n) * tm_n + lax.rem(tm - steps[e][1] + tm_n, tm_n)

    def far_copy(h, e):
        to = {"col": lax.rem(col + steps[e][0], col_n), "tm": lax.rem(tm + steps[e][1], tm_n)}
        at = columns(me, h)
        return remote(out.at[:, at], out.at[:, at], far_send.at[h, e - 1], far_recv.at[h, e - 1], to)

    def near_copy(h, e):
        at = columns(origin(e), h)
        return remote(out.at[:, at], out.at[:, at], near_send.at[h, e], near_recv.at[h, e],
                      {"col": col + 1 - 2 * lax.rem(col, 2)})

    def ridge_copy(d):
        return remote(ridge, ridges.at[col], r_send.at[d - 1], r_recv.at[d - 1], {"col": lax.rem(col + d, col_n)})

    def in_copy(c):
        return pltpu.make_async_copy(
            flat.at[:, :, pl.ds(starts[c], sizes[c])], source.at[c % 2, :, :, pl.ds(0, sizes[c])], in_sem.at[c % 2])

    def out_copy(c, s):
        to = pieces[c][s - 1] if s else own.at[:, pl.ds(starts[c], sizes[c])]
        return pltpu.make_async_copy(sorted_.at[c % 2, s, :, pl.ds(0, sizes[c])], to, out_sem.at[c % 2, s])

    def head_copy(s):
        return remote(pieces[0][s - 1], head.at[pl.ds((s - 1) * times, times)], head_send.at[s - 1],
                      head_recv.at[s - 1], {"row": lax.rem(row + s, row_n)})

    def finish(c):
        for s in range(row_n):
            out_copy(c, s).wait()

    def split(c):
        if c >= count:
            return
        in_copy(c).wait()
        if c + 1 < count:
            in_copy(c + 1).start()
        if c >= 2:
            finish(c - 2)
        for k in range(row_n):
            @pl.when(row == k)
            def _():
                def strip(t, carry):
                    at = pl.ds(pl.multiple_of(t * 16, 16), 16)
                    for s in range(row_n):
                        sorted_[c % 2, s, at, :sizes[c]] = source[c % 2, at, (k + s) % row_n, :sizes[c]]
                    return carry

                lax.fori_loop(0, times // 16, strip, 0)
        for s in range(row_n):
            out_copy(c, s).start()

    started = []

    def start(copy):
        copy.start()
        started.append(copy)

    in_copy(0).start()
    for h in range(2):
        for d in range(1, plane):
            start(sum_copy(h, d))
    for d in range(1, col_n):
        start(ridge_copy(d))
    ridges[col] = ridge[...]
    split(0)
    for h in range(2):
        total = part[:, columns(me, h)].astype(jnp.float32)
        for d in range(1, plane):
            sum_copy(h, d).wait_recv()
            total = total + summed[h, d - 1].astype(jnp.float32)
        series[h, here] = total.astype(jnp.bfloat16)
        for d in range(1, row_n):
            start(row_copy(h, d))
    split(1)
    split(2)
    for h in range(2):
        for d in range(1, row_n):
            row_copy(h, d).wait_recv()
        out[:, columns(me, h)] = mm(w[...], series[h]).astype(jnp.bfloat16)
        for e in range(1, len(steps)):
            start(far_copy(h, e))
        start(near_copy(h, 0))
    if count < 3:
        finish(0)
    for s in range(1, row_n):
        start(head_copy(s))
    split(3)
    split(4)
    for h in range(2):
        for e in range(1, len(steps)):
            far_copy(h, e).wait_recv()
            start(near_copy(h, e))
    for d in range(1, col_n):
        ridge_copy(d).wait_recv()
    for h in range(2):
        for e in range(len(steps)):
            near_copy(h, e).wait_recv()
    for c in range(max(count - 2, 1 if count < 3 else 0), count):
        finish(c)
    for s in range(1, row_n):
        head_copy(s).wait_recv()
    for copy in started:
        copy.wait_send()


def gather_slab(part, ridge, w, flat, starts, sizes, row_n, col_n, tm_n):
    times, slab = part.shape
    depth = w.shape[0]
    plane = col_n * tm_n
    wide = slab // plane // 2
    far = col_n // 2 * tm_n
    dma = pltpu.SemaphoreType.DMA
    vmem = pl.BlockSpec(memory_space=pltpu.VMEM)
    return pl.pallas_call(
        functools.partial(gather_kernel, row_n, col_n, tm_n, starts, sizes),
        out_shape=[jax.ShapeDtypeStruct((depth, slab), jnp.bfloat16),
                   jax.ShapeDtypeStruct((col_n,) + ridge.shape, jnp.float32),
                   jax.ShapeDtypeStruct((times, flat.shape[2]), flat.dtype),
                   jax.ShapeDtypeStruct(((row_n - 1) * times, sizes[0]), flat.dtype)]
        + [jax.ShapeDtypeStruct((times, n), flat.dtype) for n in sizes for _ in range(row_n - 1)],
        in_specs=[vmem] * 3 + [pl.BlockSpec(memory_space=pl.ANY)],
        out_specs=[vmem] * 2 + [pl.BlockSpec(memory_space=pl.ANY)] * (2 + len(sizes) * (row_n - 1)),
        scratch_shapes=[
            pltpu.VMEM((2, plane - 1, times, wide), jnp.bfloat16),
            pltpu.VMEM((2, depth, wide), jnp.bfloat16),
            pltpu.VMEM((2, times, row_n, max(sizes)), jnp.bfloat16),
            pltpu.VMEM((2, row_n, times, max(sizes)), jnp.bfloat16),
            dma((2, plane - 1)), dma((2, plane - 1)), dma((2, row_n - 1)), dma((2, row_n - 1)),
            dma((2, far - 1)), dma((2, far - 1)), dma((2, far)), dma((2, far)),
            dma((col_n - 1,)), dma((col_n - 1,)),
            dma((2,)), dma((2, row_n)), dma((row_n - 1,)), dma((row_n - 1,)),
        ],
        compiler_params=pltpu.CompilerParams(
            collective_id=1, has_side_effects=True, vmem_limit_bytes=60 * 2**20),
        cost_estimate=pl.CostEstimate(flops=40 * 10**9, bytes_accessed=2**20, transcendentals=0),
        name="gather_slab",
    )(part, ridge, w, flat)


def pick_kernel(rows, info, x_ref, o_ref):
    keep = info[1 + pl.program_id(0)] > 0
    for k in range(rows):
        @pl.when(keep & (info[0] == k))
        def _():
            def strip(t, carry):
                at = pl.ds(pl.multiple_of(t * 16, 16), 16)
                o_ref[at, :] = x_ref[at, k, :]
                return carry

            lax.fori_loop(0, o_ref.shape[0] // 16, strip, 0)

    @pl.when(jnp.logical_not(keep))
    def _():
        o_ref[...] = jnp.zeros_like(o_ref)


def pick_blocks(which, keep, at, x, wide):
    times, rows, _ = x.shape
    n = at.shape[0]
    info = jnp.concatenate([which.reshape(1), keep, at]).astype(jnp.int32)
    return pl.pallas_call(
        functools.partial(pick_kernel, rows),
        grid_spec=pltpu.PrefetchScalarGridSpec(
            num_scalar_prefetch=1,
            grid=(n,),
            in_specs=[pl.BlockSpec((times, rows, wide), lambda p, info: (0, 0, info[1 + n + p]))],
            out_specs=pl.BlockSpec((times, wide), lambda p, info: (0, p)),
        ),
        out_shape=jax.ShapeDtypeStruct((times, n * wide), x.dtype),
        cost_estimate=pl.CostEstimate(flops=0, bytes_accessed=2 * times * rows * n * wide * 2, transcendentals=0),
        name="pick_blocks",
    )(info, x)


def final_body(chunk_base, info, own_ref, rest_ref, p_ref, d_ref, r_ref, *rest):
    t_ref, f_ref = rest[-2:]
    _, width = t_ref.shape
    times = own_ref.shape[1]
    acc = mm(own_ref[0], p_ref[:times, :], TN) + mm(rest_ref[0], p_ref[times:, :], TN)
    kind = kind_of(info, chunk_base(pl.program_id(0), pl.program_id(1)))

    def put(first, second, last):
        f_ref[0] = first.astype(f_ref.dtype)
        f_ref[1] = second.astype(f_ref.dtype)
        t_ref[...] = last

    @pl.when(kind < 2)
    def _():
        full = acc + d_ref[...]
        put(full[:, :width], full[:, width:2 * width], full[:, 2 * width:])

    @pl.when(kind == 2)
    def _():
        put(acc[:, :width], acc[:, width:2 * width],
            acc[:, 2 * width:] + jnp.where(eye_mask(width), r_ref[...], 0.0))

    @pl.when(kind > 2)
    def _():
        put(acc[:, :width], acc[:, width:2 * width], acc[:, 2 * width:])


def kind_of(info, block):
    at = block - info[4]
    inside = (at >= 0) & (at < info[5])
    kind = jnp.where(at == info[0], 0, jnp.where(at == info[1], 1, jnp.where(at == info[2], 2, 3)))
    return jnp.where(inside, kind, 3)


def final_chunk(info, own, others, weights, d, ridge, prior, start, width):
    cols, times, local = own.shape
    bm = width
    w = others.shape[2]
    per = w // bm
    rows = cols * local
    rest = others.shape[1]

    def base(c, i):
        return c * (local // bm) + start // bm + i

    in_specs = [
        pl.BlockSpec((1, times, bm), lambda c, i, info: (c, 0, start // bm + i)),
        pl.BlockSpec((1, rest, bm), lambda c, i, info: (c, 0, i)),
        pl.BlockSpec(weights.shape, lambda c, i, info: (0, 0)),
        pl.BlockSpec((bm, 3 * width), lambda c, i, info: (jnp.where(kind_of(info, base(c, i)) == 1, 1, 0), 0)),
        pl.BlockSpec((1, width), lambda c, i, info: (0, 0)),
    ]
    operands = [info, own, others, weights, d, ridge]
    aliases = {}
    if prior is not None:
        in_specs += [pl.BlockSpec(memory_space=pl.ANY)] * 2
        aliases = {len(operands): 0, len(operands) + 1: 1}
        operands += list(prior)
    return pl.pallas_call(
        functools.partial(final_body, base),
        grid_spec=pltpu.PrefetchScalarGridSpec(
            num_scalar_prefetch=1,
            grid=(cols, per),
            in_specs=in_specs,
            out_specs=[
                pl.BlockSpec((bm, width), lambda c, i, info: (base(c, i), 0)),
                pl.BlockSpec((2, bm, width), lambda c, i, info: (0, base(c, i), 0)),
            ],
        ),
        out_shape=[
            jax.ShapeDtypeStruct((rows, width), jnp.float32),
            jax.ShapeDtypeStruct((2, rows, width), jnp.bfloat16),
        ],
        input_output_aliases=aliases,
        compiler_params=pltpu.CompilerParams(
            vmem_limit_bytes=48 * 2**20, dimension_semantics=("arbitrary", "arbitrary")
        ),
        cost_estimate=pl.CostEstimate(
            flops=2 * cols * w * (times + rest) * 3 * width, bytes_accessed=cols * w * 6 * 2**10, transcendentals=0),
        name="final",
    )(*operands)


def on_device(samples, whitening, ridge, slab_start, panels):
    times, groups, _, local = samples.shape
    rows = lax.axis_size("row")
    cols = lax.axis_size("col")
    tms = lax.axis_size("tm")
    width = ridge.shape[0]
    slab = width * cols
    kd = local * cols
    depth = whitening.shape[0]
    scale = 1.0 / math.sqrt(depth)
    me_col = lax.axis_index("col")
    me_tm = lax.axis_index("tm")
    me_row = lax.axis_index("row")

    first = slab_start[0] * slab
    group = first // (tms * kd)
    tm_owner = (first % (tms * kd)) // kd
    offset = first % kd

    flat = samples.reshape(times, groups, local)
    eighth = local // 8
    sizes = [eighth, 2 * eighth, 2 * eighth, 2 * eighth, eighth] if eighth >= width else [width] * (local // width)
    starts = [sum(sizes[:c]) for c in range(len(sizes))]
    at = offset + jnp.arange(cols) * width
    have = (me_tm == tm_owner) & (me_col == at // local)
    part = pick_blocks(group, have, at % local // width, flat, width)
    sw, ridges, own, head, *pieces = gather_slab(
        part, jnp.broadcast_to(ridge, (SUB, width)), whitening, flat, starts, sizes, rows, cols, tms)
    ridges = ridges[:, 0].reshape(1, slab)
    own = lax.all_gather(own, "col", axis=0)
    others = []
    for c in range(len(sizes)):
        block = pieces[c * (rows - 1):(c + 1) * (rows - 1)]
        if c:
            head = jnp.concatenate([
                lax.ppermute(block[s - 1], "row", [(i, (i + s) % rows) for i in range(rows)])
                for s in range(1, rows)
            ], axis=0)
        others.append(lax.all_gather(head, "col", axis=0))

    q0, q1 = panels[0], panels[1]
    owner = (me_row == group) & (me_tm == tm_owner)
    kind = jnp.where(me_col == q0, 0, jnp.where(me_col == q1, 1, 2))
    info = jnp.stack([
        q0, q1, me_col, kind, offset // width, jnp.where(owner, cols, 0), me_row,
    ]).astype(jnp.int32)
    square = jax.ShapeDtypeStruct((width, width), jnp.float32)
    coarse = jax.ShapeDtypeStruct((width, width), jnp.bfloat16)
    scratch = [pltpu.VMEM((width, 2 * width), jnp.float32), pltpu.VMEM((NB, 2 * width), jnp.float32),
               pltpu.VMEM((2, NB // SUB, SUB, SUB, NB), jnp.float32)]
    i0, = chain_call(
        functools.partial(first_kernel, scale), info, [sw, ridges], [0, 0], [square], scratch, 20 * 10**9, "first")
    c01, c0j, i1 = chain_call(
        functools.partial(second_kernel, scale), info, [sw, sw, sw, ridges, ridges, i0], [0, 1, 2, 0, 1, None],
        [coarse, coarse, square], scratch, 24 * 10**9, "second")
    weights, d = chain_call(
        functools.partial(third_kernel, scale, rows), info,
        [sw, sw, sw, ridges, ridges, i0, i1, c01, c0j, whitening], [0, 1, 2, 0, 1, None, None, None, None, None],
        [jax.ShapeDtypeStruct((depth, 3 * width), jnp.bfloat16), jax.ShapeDtypeStruct((2 * width, 3 * width), jnp.float32)],
        [], 15 * 10**9, "third")
    own_ridge = ridge.reshape(1, width) * (kind == 2).astype(jnp.float32)

    prior = None
    for c, start in enumerate(starts):
        prior = final_chunk(info, own, others[c], weights, d, own_ridge, prior, start, width)
    return tuple(prior)


def solution(mesh):
    in_specs = (P("row", None, "tm", "col"), P(), P("col"), P(), P())
    out_specs = (P(("row", "tm"), "col"), P(None, ("row", "tm"), None))
    return jax.shard_map(on_device, mesh=mesh, in_specs=in_specs, out_specs=out_specs, check_vma=False)
```

```python
import functools
import math
import jax
import jax.numpy as jnp
from jax import lax
from jax.experimental import pallas as pl
from jax.experimental.pallas import tpu as pltpu
from jax.sharding import PartitionSpec as P

NB = 128
SUB = 8
HOPS = (1, 3)
HIGH = lax.Precision.HIGHEST
MESH = pl.DeviceIdType.MESH
NN = (((1,), (0,)), ((), ()))
NT = (((1,), (1,)), ((), ()))
TN = (((0,), (0,)), ((), ()))


def spread(x):
    return jnp.broadcast_to(x, (SUB, NB))


def block_inverse(a, held):
    n = NB // SUB
    rows = [a[s * SUB:(s + 1) * SUB, :] for s in range(n)]
    lane = lax.broadcasted_iota(jnp.int32, (SUB, NB), 1)
    sub = lax.broadcasted_iota(jnp.int32, (SUB, NB), 0)
    inv = [jnp.where(lane == sub + s * SUB, 1.0, 0.0).astype(jnp.float32) for s in range(n)]
    for p in range(n):
        for s in range(p, n):
            for c in range(SUB):
                held[p % 2, s, c] = spread(rows[s][:, p * SUB + c:p * SUB + c + 1])
        cols = {s: [held[p % 2, s, c] for c in range(SUB)] for s in range(p, n)}
        for c in range(SUB):
            over = 1.0 / spread(cols[p][c][c:c + 1, :])
            row, inverse = spread(rows[p][c:c + 1, :]), spread(inv[p][c:c + 1, :])
            heads = [spread(cols[p][d][c:c + 1, :]) for d in range(c + 1, SUB)]
            for s in range(p, n):
                m = cols[s][c] * over
                if s == p:
                    m = jnp.where(sub > c, m, 0.0)
                rows[s] = rows[s] - m * row
                inv[s] = inv[s] - m * inverse
                for d, head in zip(range(c + 1, SUB), heads):
                    cols[s][d] = cols[s][d] - m * head
    out = []
    for s in range(n):
        d = jnp.sum(jnp.where(lane == sub + s * SUB, rows[s], 0.0), axis=1, keepdims=True)
        out.append(inv[s] / jnp.sqrt(d))
    return jnp.concatenate(out, axis=0)


def invert(work, top, held):
    size = work.shape[0]
    blocks = size // NB

    def step(b, carry):
        at = pl.multiple_of(b * NB, NB)
        small = block_inverse(work[pl.ds(at, NB), pl.ds(at, NB)], held)
        top[...] = jnp.dot(small, work[pl.ds(at, NB), :], preferred_element_type=jnp.float32, precision=HIGH)
        work[pl.ds(at, NB), :] = top[...]

        def lower(c, carry):
            to = pl.multiple_of(c * NB, NB)
            work[pl.ds(to, NB), :] -= lax.dot_general(
                top[:, pl.ds(to, NB)], top[...], TN, preferred_element_type=jnp.float32, precision=HIGH)
            return carry

        return lax.fori_loop(b + 1, blocks, lower, carry)

    lax.fori_loop(0, blocks, step, 0)


def eye_mask(size):
    return lax.broadcasted_iota(jnp.int32, (size, size), 0) == lax.broadcasted_iota(jnp.int32, (size, size), 1)


def mm(a, b, dims=NN):
    return lax.dot_general(a, b, dims, preferred_element_type=jnp.float32)


def halves(a):
    hi = a.astype(jnp.bfloat16)
    return hi, (a - hi.astype(jnp.float32)).astype(jnp.bfloat16)


def mm2(a, b, dims=NN):
    hi, lo = halves(a)
    return mm(lo, b, dims) + mm(hi, b, dims)


def mm3(a, b, dims=NN):
    hi, lo = halves(a)
    bhi, blo = halves(b)
    return mm(lo, bhi, dims) + mm(hi, blo, dims) + mm(hi, bhi, dims)


def first_kernel(scale, info, s0_ref, r0_ref, i0_ref, work, top, held):
    size = s0_ref.shape[1]
    eye = eye_mask(size)
    work[:, :size] = mm(s0_ref[...], s0_ref[...], TN) * scale + jnp.where(eye, r0_ref[...], 0.0)
    work[:, size:] = jnp.where(eye, 1.0, 0.0)
    invert(work, top, held)
    i0_ref[...] = work[:, size:]


def second_kernel(scale, info, s0_ref, s1_ref, sj_ref, r0_ref, r1_ref, i0_ref, c01_ref, c0j_ref, i1_ref, work, top, held):
    size = s0_ref.shape[1]
    eye = eye_mask(size)
    i0 = i0_ref[...]
    c01 = mm3(i0, mm(s0_ref[...], s1_ref[...], TN) * scale).astype(jnp.bfloat16)
    c01_ref[...] = c01
    r0 = r0_ref[...] * (info[3] == 0).astype(jnp.float32)
    c0j_ref[...] = mm3(i0, mm(s0_ref[...], sj_ref[...], TN) * scale + jnp.where(eye, r0, 0.0)).astype(jnp.bfloat16)
    work[:, :size] = mm(s1_ref[...], s1_ref[...], TN) * scale + jnp.where(eye, r1_ref[...], 0.0) - mm(c01, c01, TN)
    work[:, size:] = jnp.where(eye, 1.0, 0.0)
    invert(work, top, held)
    i1_ref[...] = work[:, size:]


def third_kernel(
    scale, rows, info, s0_ref, s1_ref, sj_ref, r0_ref, r1_ref, i0_ref, i1_ref, c01_ref, c0j_ref, w_ref, p_ref, d_ref
):
    size = s0_ref.shape[1]
    eye = eye_mask(size)
    live = (info[3] > 1).astype(jnp.float32)
    i0, i1, c01, c0j = i0_ref[...], i1_ref[...], c01_ref[...], c0j_ref[...]
    r1 = r1_ref[...]
    w = w_ref[...]
    times = w.shape[0] // rows

    def put(value, side):
        for t in range(rows):
            to = pl.multiple_of(lax.rem(info[6] - t + rows, rows) * times, times)
            p_ref[pl.ds(to, times), side * size:(side + 1) * size] = value[t * times:(t + 1) * times].astype(jnp.bfloat16)

    p0 = mm3(mm(w, s0_ref[...], TN) * scale, i0, NT)
    put(p0, 0)
    p1 = mm3(mm(w, s1_ref[...], TN) * scale - mm2(p0, c01), i1, NT)
    put(p1, 1)
    own = r1 * (info[3] == 1).astype(jnp.float32)
    a1j = mm(s1_ref[...], sj_ref[...], TN) * scale + jnp.where(eye, own, 0.0) - mm(c01, c0j, TN)
    c1j = mm3(i1, a1j).astype(jnp.bfloat16)
    pn = mm(w, sj_ref[...], TN) * scale - mm2(p0, c0j) - mm2(p1, c1j)
    put(pn * live, 2)
    d00 = (i0 * r0_ref[...]).T
    d10 = mm3(-mm2(d00, c01), i1, NT)
    d11 = (i1 * r1).T
    d_ref[:size, :size] = d00
    d_ref[:size, size:2 * size] = d10
    d_ref[:size, 2 * size:] = (mm2(d00, c0j) + mm2(d10, c1j)) * -live
    d_ref[size:, :size] = jnp.zeros((size, size), jnp.float32)
    d_ref[size:, size:2 * size] = d11
    d_ref[size:, 2 * size:] = mm2(d11, c1j) * -live


def chain_call(kernel, info, operands, specs, outs, scratch, flops, name):
    def spec(x, pick, width):
        if pick is None:
            return pl.BlockSpec(x.shape, lambda i, info: (0, 0))
        return pl.BlockSpec((x.shape[0], width), lambda i, info: (0, info[pick]))

    width = outs[0].shape[-1] if name != "third" else outs[0].shape[-1] // 3
    return pl.pallas_call(
        kernel,
        grid_spec=pltpu.PrefetchScalarGridSpec(
            num_scalar_prefetch=1,
            grid=(1,),
            in_specs=[spec(x, p, width) for x, p in zip(operands, specs)],
            out_specs=[pl.BlockSpec(o.shape, lambda i, info: (0, 0)) for o in outs],
            scratch_shapes=scratch,
        ),
        out_shape=outs,
        compiler_params=pltpu.CompilerParams(vmem_limit_bytes=60 * 2**20),
        cost_estimate=pl.CostEstimate(flops=flops, bytes_accessed=8 * 2**20, transcendentals=0),
    )(info, *operands)


def gather_kernel(row_n, col_n, tm_n, starts, sizes, part, ridge, w, flat, out, ridges, own, head, *rest):
    count = len(sizes)
    pieces = [rest[c * (row_n - 1):(c + 1) * (row_n - 1)] for c in range(count)]
    (summed, series, source, sorted_, sum_send, sum_recv, row_send, row_recv, far_send, far_recv, near_send, near_recv,
     r_send, r_recv, in_sem, out_sem, head_send, head_recv) = rest[count * (row_n - 1):]
    row, col, tm = lax.axis_index("row"), lax.axis_index("col"), lax.axis_index("tm")
    plane = col_n * tm_n
    me = col * tm_n + tm
    times = part.shape[0]
    here = pl.ds(pl.multiple_of(row * times, times), times)
    share = out.shape[1] // plane
    wide = share // 2

    def member(distance):
        other = lax.rem(me + distance, plane)
        return {"col": other // tm_n, "tm": lax.rem(other, tm_n)}

    def columns(owner, h):
        return pl.ds(pl.multiple_of(owner * share + h * wide, wide), wide)

    barrier = pltpu.get_barrier_semaphore()
    for d in range(1, plane):
        pl.semaphore_signal(barrier, inc=1, device_id=member(d), device_id_type=MESH)
    for d in range(1, row_n):
        pl.semaphore_signal(barrier, inc=1, device_id={"row": lax.rem(row + d, row_n)}, device_id_type=MESH)
    pl.semaphore_wait(barrier, plane + row_n - 2)

    def remote(src, dst, send, recv, to):
        return pltpu.make_async_remote_copy(
            src_ref=src, dst_ref=dst, send_sem=send, recv_sem=recv, device_id=to, device_id_type=MESH)

    def sum_copy(h, d):
        return remote(part.at[:, columns(lax.rem(me + d, plane), h)], summed.at[h, d - 1],
                      sum_send.at[h, d - 1], sum_recv.at[h, d - 1], member(d))

    def row_copy(h, d):
        return remote(series.at[h, here], series.at[h, here],
                      row_send.at[h, d - 1], row_recv.at[h, d - 1], {"row": lax.rem(row + d, row_n)})

    steps = [(a, b) for a in range(0, col_n, 2) for b in range(tm_n)]

    def origin(e):
        return lax.rem(col - steps[e][0] + col_n, col_n) * tm_n + lax.rem(tm - steps[e][1] + tm_n, tm_n)

    def far_copy(h, e):
        to = {"col": lax.rem(col + steps[e][0], col_n), "tm": lax.rem(tm + steps[e][1], tm_n)}
        at = columns(me, h)
        return remote(out.at[:, at], out.at[:, at], far_send.at[h, e - 1], far_recv.at[h, e - 1], to)

    def near_copy(h, e):
        at = columns(origin(e), h)
        return remote(out.at[:, at], out.at[:, at], near_send.at[h, e], near_recv.at[h, e],
                      {"col": col + 1 - 2 * lax.rem(col, 2)})

    def ridge_copy(d):
        return remote(ridge, ridges.at[col], r_send.at[d - 1], r_recv.at[d - 1], {"col": lax.rem(col + d, col_n)})

    def in_copy(c):
        return pltpu.make_async_copy(
            flat.at[:, :, pl.ds(starts[c], sizes[c])], source.at[c % 2, :, :, pl.ds(0, sizes[c])], in_sem.at[c % 2])

    def out_copy(c, s):
        to = pieces[c][s - 1] if s else own.at[:, pl.ds(starts[c], sizes[c])]
        return pltpu.make_async_copy(sorted_.at[c % 2, s, :, pl.ds(0, sizes[c])], to, out_sem.at[c % 2, s])

    def head_copy(s):
        return remote(pieces[0][s - 1], head.at[pl.ds((s - 1) * times, times)], head_send.at[s - 1],
                      head_recv.at[s - 1], {"row": lax.rem(row + s, row_n)})

    def finish(c):
        for s in range(row_n):
            out_copy(c, s).wait()

    def split(c):
        if c >= count:
            return
        in_copy(c).wait()
        if c + 1 < count:
            in_copy(c + 1).start()
        if c >= 2:
            finish(c - 2)
        for k in range(row_n):
            @pl.when(row == k)
            def _():
                def strip(t, carry):
                    at = pl.ds(pl.multiple_of(t * 16, 16), 16)
                    for s in range(row_n):
                        sorted_[c % 2, s, at, :sizes[c]] = source[c % 2, at, (k + s) % row_n, :sizes[c]]
                    return carry

                lax.fori_loop(0, times // 16, strip, 0)
        for s in range(row_n):
            out_copy(c, s).start()

    started = []

    def start(copy):
        copy.start()
        started.append(copy)

    in_copy(0).start()
    for h in range(2):
        for d in range(1, plane):
            start(sum_copy(h, d))
    for d in range(1, col_n):
        start(ridge_copy(d))
    ridges[col] = ridge[...]
    split(0)
    for h in range(2):
        total = part[:, columns(me, h)].astype(jnp.float32)
        for d in range(1, plane):
            sum_copy(h, d).wait_recv()
            total = total + summed[h, d - 1].astype(jnp.float32)
        series[h, here] = total.astype(jnp.bfloat16)
        for d in range(1, row_n):
            start(row_copy(h, d))
    split(1)
    split(2)
    for h in range(2):
        for d in range(1, row_n):
            row_copy(h, d).wait_recv()
        out[:, columns(me, h)] = mm(w[...], series[h]).astype(jnp.bfloat16)
        for e in range(1, len(steps)):
            start(far_copy(h, e))
        start(near_copy(h, 0))
    if count < 3:
        finish(0)
    for s in range(1, row_n):
        start(head_copy(s))
    split(3)
    split(4)
    for h in range(2):
        for e in range(1, len(steps)):
            far_copy(h, e).wait_recv()
            start(near_copy(h, e))
    for d in range(1, col_n):
        ridge_copy(d).wait_recv()
    for h in range(2):
        for e in range(len(steps)):
            near_copy(h, e).wait_recv()
    for c in range(max(count - 2, 1 if count < 3 else 0), count):
        finish(c)
    for s in range(1, row_n):
        head_copy(s).wait_recv()
    for copy in started:
        copy.wait_send()


def gather_slab(part, ridge, w, flat, starts, sizes, row_n, col_n, tm_n):
    times, slab = part.shape
    depth = w.shape[0]
    plane = col_n * tm_n
    wide = slab // plane // 2
    far = col_n // 2 * tm_n
    dma = pltpu.SemaphoreType.DMA
    vmem = pl.BlockSpec(memory_space=pltpu.VMEM)
    return pl.pallas_call(
        functools.partial(gather_kernel, row_n, col_n, tm_n, starts, sizes),
        out_shape=[jax.ShapeDtypeStruct((depth, slab), jnp.bfloat16),
                   jax.ShapeDtypeStruct((col_n,) + ridge.shape, jnp.float32),
                   jax.ShapeDtypeStruct((times, flat.shape[2]), flat.dtype),
                   jax.ShapeDtypeStruct(((row_n - 1) * times, sizes[0]), flat.dtype)]
        + [jax.ShapeDtypeStruct((times, n), flat.dtype) for n in sizes for _ in range(row_n - 1)],
        in_specs=[vmem] * 3 + [pl.BlockSpec(memory_space=pl.ANY)],
        out_specs=[vmem] * 2 + [pl.BlockSpec(memory_space=pl.ANY)] * (2 + len(sizes) * (row_n - 1)),
        scratch_shapes=[
            pltpu.VMEM((2, plane - 1, times, wide), jnp.bfloat16),
            pltpu.VMEM((2, depth, wide), jnp.bfloat16),
            pltpu.VMEM((2, times, row_n, max(sizes)), jnp.bfloat16),
            pltpu.VMEM((2, row_n, times, max(sizes)), jnp.bfloat16),
            dma((2, plane - 1)), dma((2, plane - 1)), dma((2, row_n - 1)), dma((2, row_n - 1)),
            dma((2, far - 1)), dma((2, far - 1)), dma((2, far)), dma((2, far)),
            dma((col_n - 1,)), dma((col_n - 1,)),
            dma((2,)), dma((2, row_n)), dma((row_n - 1,)), dma((row_n - 1,)),
        ],
        compiler_params=pltpu.CompilerParams(
            collective_id=1, has_side_effects=True, vmem_limit_bytes=60 * 2**20),
        cost_estimate=pl.CostEstimate(flops=40 * 10**9, bytes_accessed=2**20, transcendentals=0),
        name="gather_slab",
    )(part, ridge, w, flat)


def pick_kernel(rows, info, x_ref, o_ref):
    keep = info[1 + pl.program_id(0)] > 0
    for k in range(rows):
        @pl.when(keep & (info[0] == k))
        def _():
            def strip(t, carry):
                at = pl.ds(pl.multiple_of(t * 16, 16), 16)
                o_ref[at, :] = x_ref[at, k, :]
                return carry

            lax.fori_loop(0, o_ref.shape[0] // 16, strip, 0)

    @pl.when(jnp.logical_not(keep))
    def _():
        o_ref[...] = jnp.zeros_like(o_ref)


def pick_blocks(which, keep, at, x, wide):
    times, rows, _ = x.shape
    n = at.shape[0]
    info = jnp.concatenate([which.reshape(1), keep, at]).astype(jnp.int32)
    return pl.pallas_call(
        functools.partial(pick_kernel, rows),
        grid_spec=pltpu.PrefetchScalarGridSpec(
            num_scalar_prefetch=1,
            grid=(n,),
            in_specs=[pl.BlockSpec((times, rows, wide), lambda p, info: (0, 0, info[1 + n + p]))],
            out_specs=pl.BlockSpec((times, wide), lambda p, info: (0, p)),
        ),
        out_shape=jax.ShapeDtypeStruct((times, n * wide), x.dtype),
        cost_estimate=pl.CostEstimate(flops=0, bytes_accessed=2 * times * rows * n * wide * 2, transcendentals=0),
        name="pick_blocks",
    )(info, x)


def final_body(chunk_base, units, info, own_ref, *refs):
    p_ref, d_ref, r_ref = refs[units:units + 3]
    rest_ref = refs[0]
    if units > 1:
        t_ref, f_ref, rest_ref = refs[-3:]
        for u in range(units):
            @pl.when(pl.program_id(0) == u)
            def _():
                rest_ref[0] = refs[u][...]
    else:
        t_ref, f_ref = refs[-2:]
    _, width = t_ref.shape
    times = own_ref.shape[1]
    acc = mm(own_ref[0], p_ref[:times, :], TN) + mm(rest_ref[0], p_ref[times:, :], TN)
    kind = kind_of(info, chunk_base(pl.program_id(0), pl.program_id(1), info))

    def put(first, second, last):
        f_ref[0] = first.astype(f_ref.dtype)
        f_ref[1] = second.astype(f_ref.dtype)
        t_ref[...] = last

    @pl.when(kind < 2)
    def _():
        full = acc + d_ref[...]
        put(full[:, :width], full[:, width:2 * width], full[:, 2 * width:])

    @pl.when(kind == 2)
    def _():
        put(acc[:, :width], acc[:, width:2 * width],
            acc[:, 2 * width:] + jnp.where(eye_mask(width), r_ref[...], 0.0))

    @pl.when(kind > 2)
    def _():
        put(acc[:, :width], acc[:, width:2 * width], acc[:, 2 * width:])


def kind_of(info, block):
    at = block - info[4]
    inside = (at >= 0) & (at < info[5])
    kind = jnp.where(at == info[0], 0, jnp.where(at == info[1], 1, jnp.where(at == info[2], 2, 3)))
    return jnp.where(inside, kind, 3)


def final_chunk(info, own, others, weights, d, ridge, prior, start, width):
    cols, times, local = own.shape
    bm = width
    units = len(others)
    w = others[0].shape[-1]
    rest = others[0].shape[-2]
    per = w // bm
    rows = cols * local

    def column(c, info):
        if units == 1:
            return c
        far, bits = 0, units.bit_length() - 1
        for b in range(bits):
            far = far + (((c >> b) & 1) << (bits - 1 - b))
        return info[2] ^ far

    def base(c, i, info):
        return column(c, info) * (local // bm) + start // bm + i

    def unit_spec(u):
        if units == 1:
            return pl.BlockSpec((1, rest, bm), lambda c, i, info: (c, 0, i))
        return pl.BlockSpec((rest, bm), lambda c, i, info: (0, jnp.where(c == u, i, jnp.where(c > u, per - 1, 0))))

    in_specs = [
        pl.BlockSpec((1, times, bm), lambda c, i, info: (column(c, info), 0, start // bm + i)),
        *[unit_spec(u) for u in range(units)],
        pl.BlockSpec(weights.shape, lambda c, i, info: (0, 0)),
        pl.BlockSpec((bm, 3 * width), lambda c, i, info: (jnp.where(kind_of(info, base(c, i, info)) == 1, 1, 0), 0)),
        pl.BlockSpec((1, width), lambda c, i, info: (0, 0)),
    ]
    operands = [info, own, *others, weights, d, ridge]
    aliases = {}
    if prior is not None:
        in_specs += [pl.BlockSpec(memory_space=pl.ANY)] * 2
        aliases = {len(operands): 0, len(operands) + 1: 1}
        operands += list(prior)
    return pl.pallas_call(
        functools.partial(final_body, base, units),
        grid_spec=pltpu.PrefetchScalarGridSpec(
            num_scalar_prefetch=1,
            grid=(cols, per),
            in_specs=in_specs,
            out_specs=[
                pl.BlockSpec((bm, width), lambda c, i, info: (base(c, i, info), 0)),
                pl.BlockSpec((2, bm, width), lambda c, i, info: (0, base(c, i, info), 0)),
            ],
            scratch_shapes=[pltpu.VMEM((1, rest, bm), jnp.bfloat16)] if units > 1 else [],
        ),
        out_shape=[
            jax.ShapeDtypeStruct((rows, width), jnp.float32),
            jax.ShapeDtypeStruct((2, rows, width), jnp.bfloat16),
        ],
        input_output_aliases=aliases,
        compiler_params=pltpu.CompilerParams(
            vmem_limit_bytes=48 * 2**20, dimension_semantics=("arbitrary", "arbitrary")
        ),
        cost_estimate=pl.CostEstimate(
            flops=2 * cols * w * (times + rest) * 3 * width, bytes_accessed=cols * w * 6 * 2**10, transcendentals=0),
        name="final",
    )(*operands)


def hop_gather(block, cols):
    held = [block]
    bit = cols // 2
    while bit:
        held = held + [lax.ppermute(h, "col", [(i, i ^ bit) for i in range(cols)]) for h in held]
        bit //= 2
    return held


def on_device(samples, whitening, ridge, slab_start, panels):
    times, groups, _, local = samples.shape
    rows = lax.axis_size("row")
    cols = lax.axis_size("col")
    tms = lax.axis_size("tm")
    width = ridge.shape[0]
    slab = width * cols
    kd = local * cols
    depth = whitening.shape[0]
    scale = 1.0 / math.sqrt(depth)
    me_col = lax.axis_index("col")
    me_tm = lax.axis_index("tm")
    me_row = lax.axis_index("row")

    first = slab_start[0] * slab
    group = first // (tms * kd)
    tm_owner = (first % (tms * kd)) // kd
    offset = first % kd

    flat = samples.reshape(times, groups, local)
    eighth = local // 8
    sizes = [eighth, 2 * eighth, 2 * eighth, 2 * eighth, eighth] if eighth >= width else [width] * (local // width)
    starts = [sum(sizes[:c]) for c in range(len(sizes))]
    at = offset + jnp.arange(cols) * width
    have = (me_tm == tm_owner) & (me_col == at // local)
    part = pick_blocks(group, have, at % local // width, flat, width)
    sw, ridges, own, head, *pieces = gather_slab(
        part, jnp.broadcast_to(ridge, (SUB, width)), whitening, flat, starts, sizes, rows, cols, tms)
    ridges = ridges[:, 0].reshape(1, slab)
    own = lax.all_gather(own, "col", axis=0)
    others = []
    hops = HOPS if len(sizes) == 5 and cols & (cols - 1) == 0 else ()
    for c in range(len(sizes)):
        block = pieces[c * (rows - 1):(c + 1) * (rows - 1)]
        if c:
            head = jnp.concatenate([
                lax.ppermute(block[s - 1], "row", [(i, (i + s) % rows) for i in range(rows)])
                for s in range(1, rows)
            ], axis=0)
        if c in hops:
            others.append(hop_gather(head, cols))
        else:
            others.append([lax.all_gather(head, "col", axis=0)])

    q0, q1 = panels[0], panels[1]
    owner = (me_row == group) & (me_tm == tm_owner)
    kind = jnp.where(me_col == q0, 0, jnp.where(me_col == q1, 1, 2))
    info = jnp.stack([
        q0, q1, me_col, kind, offset // width, jnp.where(owner, cols, 0), me_row,
    ]).astype(jnp.int32)
    square = jax.ShapeDtypeStruct((width, width), jnp.float32)
    coarse = jax.ShapeDtypeStruct((width, width), jnp.bfloat16)
    scratch = [pltpu.VMEM((width, 2 * width), jnp.float32), pltpu.VMEM((NB, 2 * width), jnp.float32),
               pltpu.VMEM((2, NB // SUB, SUB, SUB, NB), jnp.float32)]
    i0, = chain_call(
        functools.partial(first_kernel, scale), info, [sw, ridges], [0, 0], [square], scratch, 20 * 10**9, "first")
    c01, c0j, i1 = chain_call(
        functools.partial(second_kernel, scale), info, [sw, sw, sw, ridges, ridges, i0], [0, 1, 2, 0, 1, None],
        [coarse, coarse, square], scratch, 24 * 10**9, "second")
    weights, d = chain_call(
        functools.partial(third_kernel, scale, rows), info,
        [sw, sw, sw, ridges, ridges, i0, i1, c01, c0j, whitening], [0, 1, 2, 0, 1, None, None, None, None, None],
        [jax.ShapeDtypeStruct((depth, 3 * width), jnp.bfloat16), jax.ShapeDtypeStruct((2 * width, 3 * width), jnp.float32)],
        [], 15 * 10**9, "third")
    own_ridge = ridge.reshape(1, width) * (kind == 2).astype(jnp.float32)

    prior = None
    for c, start in enumerate(starts):
        prior = final_chunk(info, own, others[c], weights, d, own_ridge, prior, start, width)
    return tuple(prior)


def solution(mesh):
    in_specs = (P("row", None, "tm", "col"), P(), P("col"), P(), P())
    out_specs = (P(("row", "tm"), "col"), P(None, ("row", "tm"), None))
    return jax.shard_map(on_device, mesh=mesh, in_specs=in_specs, out_specs=out_specs, check_vma=False)
```

```python
import functools
import math
import jax
import jax.numpy as jnp
from jax import lax
from jax.experimental import pallas as pl
from jax.experimental.pallas import tpu as pltpu
from jax.sharding import PartitionSpec as P

NB = 128
SUB = 8
HIGH = lax.Precision.HIGHEST
MESH = pl.DeviceIdType.MESH
NN = (((1,), (0,)), ((), ()))
NT = (((1,), (1,)), ((), ()))
TN = (((0,), (0,)), ((), ()))


def spread(x):
    return jnp.broadcast_to(x, (SUB, NB))


def block_inverse(a, held):
    n = NB // SUB
    rows = [a[s * SUB:(s + 1) * SUB, :] for s in range(n)]
    lane = lax.broadcasted_iota(jnp.int32, (SUB, NB), 1)
    sub = lax.broadcasted_iota(jnp.int32, (SUB, NB), 0)
    inv = [jnp.where(lane == sub + s * SUB, 1.0, 0.0).astype(jnp.float32) for s in range(n)]
    for p in range(n):
        for s in range(p, n):
            for c in range(SUB):
                held[p % 2, s, c] = spread(rows[s][:, p * SUB + c:p * SUB + c + 1])
        cols = {s: [held[p % 2, s, c] for c in range(SUB)] for s in range(p, n)}
        for c in range(SUB):
            over = 1.0 / spread(cols[p][c][c:c + 1, :])
            row, inverse = spread(rows[p][c:c + 1, :]), spread(inv[p][c:c + 1, :])
            heads = [spread(cols[p][d][c:c + 1, :]) for d in range(c + 1, SUB)]
            for s in range(p, n):
                m = cols[s][c] * over
                if s == p:
                    m = jnp.where(sub > c, m, 0.0)
                rows[s] = rows[s] - m * row
                inv[s] = inv[s] - m * inverse
                for d, head in zip(range(c + 1, SUB), heads):
                    cols[s][d] = cols[s][d] - m * head
    out = []
    for s in range(n):
        d = jnp.sum(jnp.where(lane == sub + s * SUB, rows[s], 0.0), axis=1, keepdims=True)
        out.append(inv[s] / jnp.sqrt(d))
    return jnp.concatenate(out, axis=0)


def invert(work, top, held):
    size = work.shape[0]
    blocks = size // NB

    def step(b, carry):
        at = pl.multiple_of(b * NB, NB)
        small = block_inverse(work[pl.ds(at, NB), pl.ds(at, NB)], held)
        top[...] = jnp.dot(small, work[pl.ds(at, NB), :], preferred_element_type=jnp.float32, precision=HIGH)
        work[pl.ds(at, NB), :] = top[...]

        def lower(c, carry):
            to = pl.multiple_of(c * NB, NB)
            work[pl.ds(to, NB), :] -= lax.dot_general(
                top[:, pl.ds(to, NB)], top[...], TN, preferred_element_type=jnp.float32, precision=HIGH)
            return carry

        return lax.fori_loop(b + 1, blocks, lower, carry)

    lax.fori_loop(0, blocks, step, 0)


def eye_mask(size):
    return lax.broadcasted_iota(jnp.int32, (size, size), 0) == lax.broadcasted_iota(jnp.int32, (size, size), 1)


def mm(a, b, dims=NN):
    return lax.dot_general(a, b, dims, preferred_element_type=jnp.float32)


def halves(a):
    hi = a.astype(jnp.bfloat16)
    return hi, (a - hi.astype(jnp.float32)).astype(jnp.bfloat16)


def mm2(a, b, dims=NN):
    hi, lo = halves(a)
    return mm(lo, b, dims) + mm(hi, b, dims)


def mm3(a, b, dims=NN):
    hi, lo = halves(a)
    bhi, blo = halves(b)
    return mm(lo, bhi, dims) + mm(hi, blo, dims) + mm(hi, bhi, dims)


def first_kernel(scale, info, s0_ref, r0_ref, i0_ref, work, top, held):
    size = s0_ref.shape[1]
    eye = eye_mask(size)
    work[:, :size] = mm(s0_ref[...], s0_ref[...], TN) * scale + jnp.where(eye, r0_ref[...], 0.0)
    work[:, size:] = jnp.where(eye, 1.0, 0.0)
    invert(work, top, held)
    i0_ref[...] = work[:, size:]


def second_kernel(
    scale, info, s0_ref, s1_ref, sj_ref, r0_ref, r1_ref, i0_ref, c01_ref, c0j_ref, i1_ref, work, top, held
):
    size = s0_ref.shape[1]
    eye = eye_mask(size)
    r0 = r0_ref[...] * (info[3] == 0).astype(jnp.float32)
    work[:, :size] = mm(s0_ref[...], s1_ref[...], TN) * scale
    work[:, size:] = mm(s0_ref[...], sj_ref[...], TN) * scale + jnp.where(eye, r0, 0.0)

    def couple(b, carry):
        at = pl.ds(pl.multiple_of(b * NB, NB), NB)
        c01_ref[at, :] = mm3(i0_ref[at, :], work[:, :size]).astype(jnp.bfloat16)
        c0j_ref[at, :] = mm3(i0_ref[at, :], work[:, size:]).astype(jnp.bfloat16)
        return carry

    lax.fori_loop(0, size // NB, couple, 0)
    work[:, :size] = (mm(s1_ref[...], s1_ref[...], TN) * scale + jnp.where(eye, r1_ref[...], 0.0)
                      - mm(c01_ref[...], c01_ref[...], TN))
    work[:, size:] = jnp.where(eye, 1.0, 0.0)
    invert(work, top, held)
    i1_ref[...] = work[:, size:]


def third_kernel(
    scale, rows, info, s0_ref, s1_ref, sj_ref, r0_ref, r1_ref, i0_ref, i1_ref, c01_ref, c0j_ref, w_ref, p_ref, d_ref,
    c1j_ref
):
    size = s0_ref.shape[1]
    depth = w_ref.shape[0]
    times = depth // rows
    strip = max(times, size // 2)
    eye = eye_mask(size)
    live = (info[3] > 1).astype(jnp.float32)
    own = r1_ref[...] * (info[3] == 1).astype(jnp.float32)
    a1j = mm(s1_ref[...], sj_ref[...], TN) * scale + jnp.where(eye, own, 0.0) - mm(c01_ref[...], c0j_ref[...], TN)
    c1j_ref[...] = mm3(i1_ref[...], a1j).astype(jnp.bfloat16)

    def weights(b, carry):
        w = w_ref[:, pl.ds(pl.multiple_of(b * strip, strip), strip)]
        p0 = mm3(mm(w, s0_ref[...], TN) * scale, i0_ref[...], NT)
        p1 = mm3(mm(w, s1_ref[...], TN) * scale - mm2(p0, c01_ref[...]), i1_ref[...], NT)
        pn = (mm(w, sj_ref[...], TN) * scale - mm2(p0, c0j_ref[...]) - mm2(p1, c1j_ref[...])) * live
        for t in range(strip // times):
            place = lax.rem(info[6] - (b * (strip // times) + t) + rows, rows)
            to = pl.ds(pl.multiple_of(place * times, times), times)
            for side, value in enumerate((p0, p1, pn)):
                p_ref[to, side * size:(side + 1) * size] = value[t * times:(t + 1) * times].astype(jnp.bfloat16)
        return carry

    lax.fori_loop(0, depth // strip, weights, 0)
    d_ref[:size, :size] = (i0_ref[...] * r0_ref[...]).T
    d_ref[size:, :size] = jnp.zeros((size, size), jnp.float32)
    d_ref[size:, size:2 * size] = (i1_ref[...] * r1_ref[...]).T

    def ridges(b, carry):
        at = pl.ds(pl.multiple_of(b * NB, NB), NB)
        low = pl.ds(pl.multiple_of(size + b * NB, NB), NB)
        d00 = d_ref[at, :size]
        d10 = mm3(-mm2(d00, c01_ref[...]), i1_ref[...], NT)
        d_ref[at, size:2 * size] = d10
        d_ref[at, 2 * size:] = (mm2(d00, c0j_ref[...]) + mm2(d10, c1j_ref[...])) * -live
        d_ref[low, 2 * size:] = mm2(d_ref[low, size:2 * size], c1j_ref[...]) * -live
        return carry

    lax.fori_loop(0, size // NB, ridges, 0)


def chain_call(kernel, info, operands, specs, outs, scratch, flops, name):
    def spec(x, pick, width):
        if pick is None:
            return pl.BlockSpec(x.shape, lambda i, info: (0, 0))
        return pl.BlockSpec((x.shape[0], width), lambda i, info: (0, info[pick]))

    width = outs[0].shape[-1] if name != "third" else outs[0].shape[-1] // 3
    return pl.pallas_call(
        kernel,
        grid_spec=pltpu.PrefetchScalarGridSpec(
            num_scalar_prefetch=1,
            grid=(1,),
            in_specs=[spec(x, p, width) for x, p in zip(operands, specs)],
            out_specs=[pl.BlockSpec(o.shape, lambda i, info: (0, 0)) for o in outs],
            scratch_shapes=scratch,
        ),
        out_shape=outs,
        compiler_params=pltpu.CompilerParams(vmem_limit_bytes=60 * 2**20),
        cost_estimate=pl.CostEstimate(flops=flops, bytes_accessed=8 * 2**20, transcendentals=0),
    )(info, *operands)


def gather_kernel(row_n, col_n, tm_n, starts, sizes, part, ridge, w, flat, out, ridges, own, head, *rest):
    count = len(sizes)
    pieces = [rest[c * (row_n - 1):(c + 1) * (row_n - 1)] for c in range(count)]
    (summed, series, source, sorted_, sum_send, sum_recv, row_send, row_recv, far_send, far_recv, near_send, near_recv,
     r_send, r_recv, in_sem, out_sem, head_send, head_recv) = rest[count * (row_n - 1):]
    row, col, tm = lax.axis_index("row"), lax.axis_index("col"), lax.axis_index("tm")
    plane = col_n * tm_n
    me = col * tm_n + tm
    times = part.shape[0]
    here = pl.ds(pl.multiple_of(row * times, times), times)
    share = out.shape[1] // plane
    wide = share // 2

    def member(distance):
        other = lax.rem(me + distance, plane)
        return {"col": other // tm_n, "tm": lax.rem(other, tm_n)}

    def columns(owner, h):
        return pl.ds(pl.multiple_of(owner * share + h * wide, wide), wide)

    barrier = pltpu.get_barrier_semaphore()
    for d in range(1, plane):
        pl.semaphore_signal(barrier, inc=1, device_id=member(d), device_id_type=MESH)
    for d in range(1, row_n):
        pl.semaphore_signal(barrier, inc=1, device_id={"row": lax.rem(row + d, row_n)}, device_id_type=MESH)
    pl.semaphore_wait(barrier, plane + row_n - 2)

    def remote(src, dst, send, recv, to):
        return pltpu.make_async_remote_copy(
            src_ref=src, dst_ref=dst, send_sem=send, recv_sem=recv, device_id=to, device_id_type=MESH)

    def sum_copy(h, d):
        return remote(part.at[:, columns(lax.rem(me + d, plane), h)], summed.at[h, d - 1],
                      sum_send.at[h, d - 1], sum_recv.at[h, d - 1], member(d))

    def row_copy(h, d):
        return remote(series.at[h, here], series.at[h, here],
                      row_send.at[h, d - 1], row_recv.at[h, d - 1], {"row": lax.rem(row + d, row_n)})

    steps = [(a, b) for a in range(0, col_n, 2) for b in range(tm_n)]

    def origin(e):
        return lax.rem(col - steps[e][0] + col_n, col_n) * tm_n + lax.rem(tm - steps[e][1] + tm_n, tm_n)

    def far_copy(h, e):
        to = {"col": lax.rem(col + steps[e][0], col_n), "tm": lax.rem(tm + steps[e][1], tm_n)}
        at = columns(me, h)
        return remote(out.at[:, at], out.at[:, at], far_send.at[h, e - 1], far_recv.at[h, e - 1], to)

    def near_copy(h, e):
        at = columns(origin(e), h)
        return remote(out.at[:, at], out.at[:, at], near_send.at[h, e], near_recv.at[h, e],
                      {"col": col + 1 - 2 * lax.rem(col, 2)})

    def ridge_copy(d):
        return remote(ridge, ridges.at[col], r_send.at[d - 1], r_recv.at[d - 1], {"col": lax.rem(col + d, col_n)})

    def in_copy(c):
        return pltpu.make_async_copy(
            flat.at[:, :, pl.ds(starts[c], sizes[c])], source.at[c % 2, :, :, pl.ds(0, sizes[c])], in_sem.at[c % 2])

    def out_copy(c, s):
        to = pieces[c][s - 1] if s else own.at[:, pl.ds(starts[c], sizes[c])]
        return pltpu.make_async_copy(sorted_.at[c % 2, s, :, pl.ds(0, sizes[c])], to, out_sem.at[c % 2, s])

    def head_copy(s):
        return remote(pieces[0][s - 1], head.at[pl.ds((s - 1) * times, times)], head_send.at[s - 1],
                      head_recv.at[s - 1], {"row": lax.rem(row + s, row_n)})

    def finish(c):
        for s in range(row_n):
            out_copy(c, s).wait()

    def split(c):
        if c >= count:
            return
        in_copy(c).wait()
        if c + 1 < count:
            in_copy(c + 1).start()
        if c >= 2:
            finish(c - 2)
        for k in range(row_n):
            @pl.when(row == k)
            def _():
                def strip(t, carry):
                    at = pl.ds(pl.multiple_of(t * 16, 16), 16)
                    for s in range(row_n):
                        sorted_[c % 2, s, at, :sizes[c]] = source[c % 2, at, (k + s) % row_n, :sizes[c]]
                    return carry

                lax.fori_loop(0, times // 16, strip, 0)
        for s in range(row_n):
            out_copy(c, s).start()

    started = []

    def start(copy):
        copy.start()
        started.append(copy)

    in_copy(0).start()
    for h in range(2):
        for d in range(1, plane):
            start(sum_copy(h, d))
    for d in range(1, col_n):
        start(ridge_copy(d))
    ridges[col] = ridge[...]
    split(0)
    for h in range(2):
        total = part[:, columns(me, h)].astype(jnp.float32)
        for d in range(1, plane):
            sum_copy(h, d).wait_recv()
            total = total + summed[h, d - 1].astype(jnp.float32)
        series[h, here] = total.astype(jnp.bfloat16)
        for d in range(1, row_n):
            start(row_copy(h, d))
    split(1)
    split(2)
    for h in range(2):
        for d in range(1, row_n):
            row_copy(h, d).wait_recv()
        out[:, columns(me, h)] = mm(w[...], series[h]).astype(jnp.bfloat16)
        for e in range(1, len(steps)):
            start(far_copy(h, e))
        start(near_copy(h, 0))
    if count < 3:
        finish(0)
    for s in range(1, row_n):
        start(head_copy(s))
    split(3)
    split(4)
    for h in range(2):
        for e in range(1, len(steps)):
            far_copy(h, e).wait_recv()
            start(near_copy(h, e))
    for d in range(1, col_n):
        ridge_copy(d).wait_recv()
    for h in range(2):
        for e in range(len(steps)):
            near_copy(h, e).wait_recv()
    for c in range(max(count - 2, 1 if count < 3 else 0), count):
        finish(c)
    for s in range(1, row_n):
        head_copy(s).wait_recv()
    for copy in started:
        copy.wait_send()


def gather_slab(part, ridge, w, flat, starts, sizes, row_n, col_n, tm_n):
    times, slab = part.shape
    depth = w.shape[0]
    plane = col_n * tm_n
    wide = slab // plane // 2
    far = col_n // 2 * tm_n
    dma = pltpu.SemaphoreType.DMA
    vmem = pl.BlockSpec(memory_space=pltpu.VMEM)
    return pl.pallas_call(
        functools.partial(gather_kernel, row_n, col_n, tm_n, starts, sizes),
        out_shape=[jax.ShapeDtypeStruct((depth, slab), jnp.bfloat16),
                   jax.ShapeDtypeStruct((col_n,) + ridge.shape, jnp.float32),
                   jax.ShapeDtypeStruct((times, flat.shape[2]), flat.dtype),
                   jax.ShapeDtypeStruct(((row_n - 1) * times, sizes[0]), flat.dtype)]
        + [jax.ShapeDtypeStruct((times, n), flat.dtype) for n in sizes for _ in range(row_n - 1)],
        in_specs=[vmem] * 3 + [pl.BlockSpec(memory_space=pl.ANY)],
        out_specs=[vmem] * 2 + [pl.BlockSpec(memory_space=pl.ANY)] * (2 + len(sizes) * (row_n - 1)),
        scratch_shapes=[
            pltpu.VMEM((2, plane - 1, times, wide), jnp.bfloat16),
            pltpu.VMEM((2, depth, wide), jnp.bfloat16),
            pltpu.VMEM((2, times, row_n, max(sizes)), jnp.bfloat16),
            pltpu.VMEM((2, row_n, times, max(sizes)), jnp.bfloat16),
            dma((2, plane - 1)), dma((2, plane - 1)), dma((2, row_n - 1)), dma((2, row_n - 1)),
            dma((2, far - 1)), dma((2, far - 1)), dma((2, far)), dma((2, far)),
            dma((col_n - 1,)), dma((col_n - 1,)),
            dma((2,)), dma((2, row_n)), dma((row_n - 1,)), dma((row_n - 1,)),
        ],
        compiler_params=pltpu.CompilerParams(
            collective_id=1, has_side_effects=True, vmem_limit_bytes=60 * 2**20),
        cost_estimate=pl.CostEstimate(flops=40 * 10**9, bytes_accessed=2**20, transcendentals=0),
        name="gather_slab",
    )(part, ridge, w, flat)


def pick_kernel(rows, info, x_ref, o_ref):
    keep = info[1 + pl.program_id(0)] > 0
    for k in range(rows):
        @pl.when(keep & (info[0] == k))
        def _():
            def strip(t, carry):
                at = pl.ds(pl.multiple_of(t * 16, 16), 16)
                o_ref[at, :] = x_ref[at, k, :]
                return carry

            lax.fori_loop(0, o_ref.shape[0] // 16, strip, 0)

    @pl.when(jnp.logical_not(keep))
    def _():
        o_ref[...] = jnp.zeros_like(o_ref)


def pick_blocks(which, keep, at, x, wide):
    times, rows, _ = x.shape
    n = at.shape[0]
    info = jnp.concatenate([which.reshape(1), keep, at]).astype(jnp.int32)
    return pl.pallas_call(
        functools.partial(pick_kernel, rows),
        grid_spec=pltpu.PrefetchScalarGridSpec(
            num_scalar_prefetch=1,
            grid=(n,),
            in_specs=[pl.BlockSpec((times, rows, wide), lambda p, info: (0, 0, info[1 + n + p]))],
            out_specs=pl.BlockSpec((times, wide), lambda p, info: (0, p)),
        ),
        out_shape=jax.ShapeDtypeStruct((times, n * wide), x.dtype),
        cost_estimate=pl.CostEstimate(flops=0, bytes_accessed=2 * times * rows * n * wide * 2, transcendentals=0),
        name="pick_blocks",
    )(info, x)


def final_body(chunk_base, units, per, start, info, *refs):
    owns, others = refs[:units], refs[units:2 * units]
    p_ref, d_ref, r_ref = refs[2 * units:2 * units + 3]
    t_ref, f_ref, held, arrived = refs[-4:]
    bm, width = t_ref.shape
    times = owns[0].shape[0]
    step = pl.program_id(0) * per + pl.program_id(1)
    slot = step % 2

    def copies(u, i, slot):
        return (
            pltpu.make_async_copy(
                owns[u].at[:, pl.ds(pl.multiple_of(start + i * bm, bm), bm)], held.at[slot, pl.ds(0, times)],
                arrived.at[slot, 0]),
            pltpu.make_async_copy(
                others[u].at[:, pl.ds(pl.multiple_of(i * bm, bm), bm)],
                held.at[slot, pl.ds(times, held.shape[1] - times)], arrived.at[slot, 1]),
        )

    def fetch(n):
        for u in range(units):
            @pl.when(n // per == u)
            def _():
                for copy in copies(u, n % per, n % 2):
                    copy.start()

    @pl.when(step == 0)
    def _():
        fetch(step)

    @pl.when(step + 1 < units * per)
    def _():
        fetch(step + 1)

    for copy in copies(0, 0, slot):
        copy.wait()
    acc = mm(held[slot], p_ref[...], TN)
    kind = kind_of(info, chunk_base(pl.program_id(0), pl.program_id(1), info))

    def put(first, second, last):
        f_ref[0] = first.astype(f_ref.dtype)
        f_ref[1] = second.astype(f_ref.dtype)
        t_ref[...] = last

    @pl.when(kind < 2)
    def _():
        full = acc + d_ref[...]
        put(full[:, :width], full[:, width:2 * width], full[:, 2 * width:])

    @pl.when(kind == 2)
    def _():
        put(acc[:, :width], acc[:, width:2 * width],
            acc[:, 2 * width:] + jnp.where(eye_mask(width), r_ref[...], 0.0))

    @pl.when(kind > 2)
    def _():
        put(acc[:, :width], acc[:, width:2 * width], acc[:, 2 * width:])


def kind_of(info, block):
    at = block - info[4]
    inside = (at >= 0) & (at < info[5])
    kind = jnp.where(at == info[0], 0, jnp.where(at == info[1], 1, jnp.where(at == info[2], 2, 3)))
    return jnp.where(inside, kind, 3)


def final_chunk(info, own, others, weights, d, ridge, prior, start, width):
    units = len(others)
    times, local = own[0].shape
    rest, w = others[0].shape
    bm = width
    per = w // bm
    rows = units * local

    def base(c, i, info):
        far, bits = 0, units.bit_length() - 1
        for b in range(bits):
            far = far + (((c >> b) & 1) << (bits - 1 - b))
        return (info[2] ^ far) * (local // bm) + start // bm + i

    in_specs = [pl.BlockSpec(memory_space=pl.ANY)] * (2 * units) + [
        pl.BlockSpec(weights.shape, lambda c, i, info: (0, 0)),
        pl.BlockSpec((bm, 3 * width), lambda c, i, info: (jnp.where(kind_of(info, base(c, i, info)) == 1, 1, 0), 0)),
        pl.BlockSpec((1, width), lambda c, i, info: (0, 0)),
    ]
    operands = [info, *own, *others, weights, d, ridge]
    aliases = {}
    if prior is not None:
        in_specs += [pl.BlockSpec(memory_space=pl.ANY)] * 2
        aliases = {len(operands): 0, len(operands) + 1: 1}
        operands += list(prior)
    return pl.pallas_call(
        functools.partial(final_body, base, units, per, start),
        grid_spec=pltpu.PrefetchScalarGridSpec(
            num_scalar_prefetch=1,
            grid=(units, per),
            in_specs=in_specs,
            out_specs=[
                pl.BlockSpec((bm, width), lambda c, i, info: (base(c, i, info), 0)),
                pl.BlockSpec((2, bm, width), lambda c, i, info: (0, base(c, i, info), 0)),
            ],
            scratch_shapes=[pltpu.VMEM((2, times + rest, bm), jnp.bfloat16), pltpu.SemaphoreType.DMA((2, 2))],
        ),
        out_shape=[
            jax.ShapeDtypeStruct((rows, width), jnp.float32),
            jax.ShapeDtypeStruct((2, rows, width), jnp.bfloat16),
        ],
        input_output_aliases=aliases,
        compiler_params=pltpu.CompilerParams(
            vmem_limit_bytes=48 * 2**20, dimension_semantics=("arbitrary", "arbitrary")
        ),
        cost_estimate=pl.CostEstimate(
            flops=2 * units * w * (times + rest) * 3 * width, bytes_accessed=units * w * 6 * 2**10, transcendentals=0),
        name="final",
    )(*operands)


def hop_gather(block, cols):
    held = [block]
    bit = cols // 2
    while bit:
        moved = []
        for h in held:
            moved.append(lax.ppermute(h, "col", [(i, i ^ bit) for i in range(cols)]))
        held = held + moved
        bit //= 2
    return held


def on_device(samples, whitening, ridge, slab_start, panels):
    times, groups, _, local = samples.shape
    rows = lax.axis_size("row")
    cols = lax.axis_size("col")
    tms = lax.axis_size("tm")
    width = ridge.shape[0]
    slab = width * cols
    kd = local * cols
    depth = whitening.shape[0]
    scale = 1.0 / math.sqrt(depth)
    me_col = lax.axis_index("col")
    me_tm = lax.axis_index("tm")
    me_row = lax.axis_index("row")

    first = slab_start[0] * slab
    group = first // (tms * kd)
    tm_owner = (first % (tms * kd)) // kd
    offset = first % kd

    flat = samples.reshape(times, groups, local)
    eighth = local // 8
    sizes = [eighth, 2 * eighth, 2 * eighth, 2 * eighth, eighth] if eighth >= width else [width] * (local // width)
    starts = [sum(sizes[:c]) for c in range(len(sizes))]
    at = offset + jnp.arange(cols) * width
    have = (me_tm == tm_owner) & (me_col == at // local)
    part = pick_blocks(group, have, at % local // width, flat, width)
    sw, ridges, own, head, *pieces = gather_slab(
        part, jnp.broadcast_to(ridge, (SUB, width)), whitening, flat, starts, sizes, rows, cols, tms)
    ridges = ridges[:, 0].reshape(1, slab)
    own = hop_gather(own, cols)
    others = []
    for c in range(len(sizes)):
        block = pieces[c * (rows - 1):(c + 1) * (rows - 1)]
        if c:
            head = jnp.concatenate([
                lax.ppermute(block[s - 1], "row", [(i, (i + s) % rows) for i in range(rows)])
                for s in range(1, rows)
            ], axis=0)
        others.append(hop_gather(head, cols))

    q0, q1 = panels[0], panels[1]
    owner = (me_row == group) & (me_tm == tm_owner)
    kind = jnp.where(me_col == q0, 0, jnp.where(me_col == q1, 1, 2))
    info = jnp.stack([
        q0, q1, me_col, kind, offset // width, jnp.where(owner, cols, 0), me_row,
    ]).astype(jnp.int32)
    square = jax.ShapeDtypeStruct((width, width), jnp.float32)
    coarse = jax.ShapeDtypeStruct((width, width), jnp.bfloat16)
    scratch = [pltpu.VMEM((width, 2 * width), jnp.float32), pltpu.VMEM((NB, 2 * width), jnp.float32),
               pltpu.VMEM((2, NB // SUB, SUB, SUB, NB), jnp.float32)]
    i0, = chain_call(
        functools.partial(first_kernel, scale), info, [sw, ridges], [0, 0], [square], scratch, 20 * 10**9, "first")
    c01, c0j, i1 = chain_call(
        functools.partial(second_kernel, scale), info, [sw, sw, sw, ridges, ridges, i0], [0, 1, 2, 0, 1, None],
        [coarse, coarse, square], scratch, 24 * 10**9, "second")
    weights, d = chain_call(
        functools.partial(third_kernel, scale, rows), info,
        [sw, sw, sw, ridges, ridges, i0, i1, c01, c0j, whitening], [0, 1, 2, 0, 1, None, None, None, None, None],
        [jax.ShapeDtypeStruct((depth, 3 * width), jnp.bfloat16), jax.ShapeDtypeStruct((2 * width, 3 * width), jnp.float32)],
        [pltpu.VMEM((width, width), jnp.bfloat16)], 15 * 10**9, "third")
    own_ridge = ridge.reshape(1, width) * (kind == 2).astype(jnp.float32)

    prior = None
    for c, start in enumerate(starts):
        prior = final_chunk(info, own, others[c], weights, d, own_ridge, prior, start, width)
    return tuple(prior)


def solution(mesh):
    in_specs = (P("row", None, "tm", "col"), P(), P("col"), P(), P())
    out_specs = (P(("row", "tm"), "col"), P(None, ("row", "tm"), None))
    return jax.shard_map(on_device, mesh=mesh, in_specs=in_specs, out_specs=out_specs, check_vma=False)
```

```python
import functools
import math
import jax
import jax.numpy as jnp
from jax import lax
from jax.experimental import pallas as pl
from jax.experimental.pallas import tpu as pltpu
from jax.sharding import PartitionSpec as P

NB = 128
SUB = 8
HIGH = lax.Precision.HIGHEST
MESH = pl.DeviceIdType.MESH
NN = (((1,), (0,)), ((), ()))
NT = (((1,), (1,)), ((), ()))
TN = (((0,), (0,)), ((), ()))


def spread(x):
    return jnp.broadcast_to(x, (SUB, NB))


def block_inverse(a, held):
    n = NB // SUB
    rows = [a[s * SUB:(s + 1) * SUB, :] for s in range(n)]
    lane = lax.broadcasted_iota(jnp.int32, (SUB, NB), 1)
    sub = lax.broadcasted_iota(jnp.int32, (SUB, NB), 0)
    inv = [jnp.where(lane == sub + s * SUB, 1.0, 0.0).astype(jnp.float32) for s in range(n)]
    for p in range(n):
        for s in range(p, n):
            for c in range(SUB):
                held[p % 2, s, c] = spread(rows[s][:, p * SUB + c:p * SUB + c + 1])
        cols = {s: [held[p % 2, s, c] for c in range(SUB)] for s in range(p, n)}
        for c in range(SUB):
            over = 1.0 / spread(cols[p][c][c:c + 1, :])
            row, inverse = spread(rows[p][c:c + 1, :]), spread(inv[p][c:c + 1, :])
            heads = [spread(cols[p][d][c:c + 1, :]) for d in range(c + 1, SUB)]
            for s in range(p, n):
                m = cols[s][c] * over
                if s == p:
                    m = jnp.where(sub > c, m, 0.0)
                rows[s] = rows[s] - m * row
                inv[s] = inv[s] - m * inverse
                for d, head in zip(range(c + 1, SUB), heads):
                    cols[s][d] = cols[s][d] - m * head
    out = []
    for s in range(n):
        d = jnp.sum(jnp.where(lane == sub + s * SUB, rows[s], 0.0), axis=1, keepdims=True)
        out.append(inv[s] / jnp.sqrt(d))
    return jnp.concatenate(out, axis=0)


def invert(work, top, held):
    size = work.shape[0]
    blocks = size // NB

    def step(b, carry):
        at = pl.multiple_of(b * NB, NB)
        small = block_inverse(work[pl.ds(at, NB), pl.ds(at, NB)], held)
        top[...] = jnp.dot(small, work[pl.ds(at, NB), :], preferred_element_type=jnp.float32, precision=HIGH)
        work[pl.ds(at, NB), :] = top[...]

        def lower(c, carry):
            to = pl.multiple_of(c * NB, NB)
            work[pl.ds(to, NB), :] -= lax.dot_general(
                top[:, pl.ds(to, NB)], top[...], TN, preferred_element_type=jnp.float32, precision=HIGH)
            return carry

        return lax.fori_loop(b + 1, blocks, lower, carry)

    lax.fori_loop(0, blocks, step, 0)


def eye_mask(size):
    return lax.broadcasted_iota(jnp.int32, (size, size), 0) == lax.broadcasted_iota(jnp.int32, (size, size), 1)


def mm(a, b, dims=NN):
    return lax.dot_general(a, b, dims, preferred_element_type=jnp.float32)


def halves(a):
    hi = a.astype(jnp.bfloat16)
    return hi, (a - hi.astype(jnp.float32)).astype(jnp.bfloat16)


def mm2(a, b, dims=NN):
    hi, lo = halves(a)
    return mm(lo, b, dims) + mm(hi, b, dims)


def mm3(a, b, dims=NN):
    hi, lo = halves(a)
    bhi, blo = halves(b)
    return mm(lo, bhi, dims) + mm(hi, blo, dims) + mm(hi, bhi, dims)


def first_kernel(scale, info, s0_ref, r0_ref, i0_ref, work, top, held):
    size = s0_ref.shape[1]
    eye = eye_mask(size)
    work[:, :size] = mm(s0_ref[...], s0_ref[...], TN) * scale + jnp.where(eye, r0_ref[...], 0.0)
    work[:, size:] = jnp.where(eye, 1.0, 0.0)
    invert(work, top, held)
    i0_ref[...] = work[:, size:]


def second_kernel(
    scale, info, s0_ref, s1_ref, sj_ref, r0_ref, r1_ref, i0_ref, c01_ref, c0j_ref, i1_ref, work, top, held
):
    size = s0_ref.shape[1]
    eye = eye_mask(size)
    r0 = r0_ref[...] * (info[3] == 0).astype(jnp.float32)
    work[:, :size] = mm(s0_ref[...], s1_ref[...], TN) * scale
    work[:, size:] = mm(s0_ref[...], sj_ref[...], TN) * scale + jnp.where(eye, r0, 0.0)

    def couple(b, carry):
        at = pl.ds(pl.multiple_of(b * NB, NB), NB)
        c01_ref[at, :] = mm3(i0_ref[at, :], work[:, :size]).astype(jnp.bfloat16)
        c0j_ref[at, :] = mm3(i0_ref[at, :], work[:, size:]).astype(jnp.bfloat16)
        return carry

    lax.fori_loop(0, size // NB, couple, 0)
    work[:, :size] = (mm(s1_ref[...], s1_ref[...], TN) * scale + jnp.where(eye, r1_ref[...], 0.0)
                      - mm(c01_ref[...], c01_ref[...], TN))
    work[:, size:] = jnp.where(eye, 1.0, 0.0)
    invert(work, top, held)
    i1_ref[...] = work[:, size:]


def third_kernel(
    scale, rows, info, s0_ref, s1_ref, sj_ref, r0_ref, r1_ref, i0_ref, i1_ref, c01_ref, c0j_ref, w_ref, p_ref, d_ref,
    c1j_ref
):
    size = s0_ref.shape[1]
    depth = w_ref.shape[0]
    times = depth // rows
    strip = max(times, size // 2)
    eye = eye_mask(size)
    live = (info[3] > 1).astype(jnp.float32)
    own = r1_ref[...] * (info[3] == 1).astype(jnp.float32)
    a1j = mm(s1_ref[...], sj_ref[...], TN) * scale + jnp.where(eye, own, 0.0) - mm(c01_ref[...], c0j_ref[...], TN)
    c1j_ref[...] = mm3(i1_ref[...], a1j).astype(jnp.bfloat16)

    def weights(b, carry):
        w = w_ref[:, pl.ds(pl.multiple_of(b * strip, strip), strip)]
        p0 = mm3(mm(w, s0_ref[...], TN) * scale, i0_ref[...], NT)
        p1 = mm3(mm(w, s1_ref[...], TN) * scale - mm2(p0, c01_ref[...]), i1_ref[...], NT)
        pn = (mm(w, sj_ref[...], TN) * scale - mm2(p0, c0j_ref[...]) - mm2(p1, c1j_ref[...])) * live
        for t in range(strip // times):
            place = lax.rem(info[6] - (b * (strip // times) + t) + rows, rows)
            to = pl.ds(pl.multiple_of(place * times, times), times)
            for side, value in enumerate((p0, p1, pn)):
                p_ref[to, side * size:(side + 1) * size] = value[t * times:(t + 1) * times].astype(jnp.bfloat16)
        return carry

    lax.fori_loop(0, depth // strip, weights, 0)
    d_ref[:size, :size] = (i0_ref[...] * r0_ref[...]).T
    d_ref[size:, :size] = jnp.zeros((size, size), jnp.float32)
    d_ref[size:, size:2 * size] = (i1_ref[...] * r1_ref[...]).T

    def ridges(b, carry):
        at = pl.ds(pl.multiple_of(b * NB, NB), NB)
        low = pl.ds(pl.multiple_of(size + b * NB, NB), NB)
        d00 = d_ref[at, :size]
        d10 = mm3(-mm2(d00, c01_ref[...]), i1_ref[...], NT)
        d_ref[at, size:2 * size] = d10
        d_ref[at, 2 * size:] = (mm2(d00, c0j_ref[...]) + mm2(d10, c1j_ref[...])) * -live
        d_ref[low, 2 * size:] = mm2(d_ref[low, size:2 * size], c1j_ref[...]) * -live
        return carry

    lax.fori_loop(0, size // NB, ridges, 0)


def chain_call(kernel, info, operands, specs, outs, scratch, flops, name):
    def spec(x, pick, width):
        if pick is None:
            return pl.BlockSpec(x.shape, lambda i, info: (0, 0))
        return pl.BlockSpec((x.shape[0], width), lambda i, info: (0, info[pick]))

    width = outs[0].shape[-1] if name != "third" else outs[0].shape[-1] // 3
    return pl.pallas_call(
        kernel,
        grid_spec=pltpu.PrefetchScalarGridSpec(
            num_scalar_prefetch=1,
            grid=(1,),
            in_specs=[spec(x, p, width) for x, p in zip(operands, specs)],
            out_specs=[pl.BlockSpec(o.shape, lambda i, info: (0, 0)) for o in outs],
            scratch_shapes=scratch,
        ),
        out_shape=outs,
        compiler_params=pltpu.CompilerParams(vmem_limit_bytes=60 * 2**20),
        cost_estimate=pl.CostEstimate(flops=flops, bytes_accessed=8 * 2**20, transcendentals=0),
    )(info, *operands)


def gather_kernel(row_n, col_n, tm_n, starts, sizes, part, ridge, w, flat, out, ridges, own, head, *rest):
    count = len(sizes)
    pieces = [rest[c * (row_n - 1):(c + 1) * (row_n - 1)] for c in range(count)]
    (summed, series, source, sorted_, sum_send, sum_recv, row_send, row_recv, far_send, far_recv, near_send, near_recv,
     r_send, r_recv, in_sem, out_sem, head_send, head_recv) = rest[count * (row_n - 1):]
    row, col, tm = lax.axis_index("row"), lax.axis_index("col"), lax.axis_index("tm")
    plane = col_n * tm_n
    me = col * tm_n + tm
    times = part.shape[0]
    here = pl.ds(pl.multiple_of(row * times, times), times)
    share = out.shape[1] // plane
    wide = share // 2

    def member(distance):
        other = lax.rem(me + distance, plane)
        return {"col": other // tm_n, "tm": lax.rem(other, tm_n)}

    def columns(owner, h):
        return pl.ds(pl.multiple_of(owner * share + h * wide, wide), wide)

    barrier = pltpu.get_barrier_semaphore()
    for d in range(1, plane):
        pl.semaphore_signal(barrier, inc=1, device_id=member(d), device_id_type=MESH)
    for d in range(1, row_n):
        pl.semaphore_signal(barrier, inc=1, device_id={"row": lax.rem(row + d, row_n)}, device_id_type=MESH)
    pl.semaphore_wait(barrier, plane + row_n - 2)

    def remote(src, dst, send, recv, to):
        return pltpu.make_async_remote_copy(
            src_ref=src, dst_ref=dst, send_sem=send, recv_sem=recv, device_id=to, device_id_type=MESH)

    def sum_copy(h, d):
        return remote(part.at[:, columns(lax.rem(me + d, plane), h)], summed.at[h, d - 1],
                      sum_send.at[h, d - 1], sum_recv.at[h, d - 1], member(d))

    def row_copy(h, d):
        return remote(series.at[h, here], series.at[h, here],
                      row_send.at[h, d - 1], row_recv.at[h, d - 1], {"row": lax.rem(row + d, row_n)})

    steps = [(a, b) for a in range(0, col_n, 2) for b in range(tm_n)]

    def origin(e):
        return lax.rem(col - steps[e][0] + col_n, col_n) * tm_n + lax.rem(tm - steps[e][1] + tm_n, tm_n)

    def far_copy(h, e):
        to = {"col": lax.rem(col + steps[e][0], col_n), "tm": lax.rem(tm + steps[e][1], tm_n)}
        at = columns(me, h)
        return remote(out.at[:, at], out.at[:, at], far_send.at[h, e - 1], far_recv.at[h, e - 1], to)

    def near_copy(h, e):
        at = columns(origin(e), h)
        return remote(out.at[:, at], out.at[:, at], near_send.at[h, e], near_recv.at[h, e],
                      {"col": col + 1 - 2 * lax.rem(col, 2)})

    def ridge_copy(d):
        return remote(ridge, ridges.at[col], r_send.at[d - 1], r_recv.at[d - 1], {"col": lax.rem(col + d, col_n)})

    def in_copy(c):
        return pltpu.make_async_copy(
            flat.at[:, :, pl.ds(starts[c], sizes[c])], source.at[c % 2, :, :, pl.ds(0, sizes[c])], in_sem.at[c % 2])

    def out_copy(c, s):
        to = pieces[c][s - 1] if s else own.at[:, pl.ds(starts[c], sizes[c])]
        return pltpu.make_async_copy(sorted_.at[c % 2, s, :, pl.ds(0, sizes[c])], to, out_sem.at[c % 2, s])

    def head_copy(s):
        return remote(pieces[0][s - 1], head.at[pl.ds((s - 1) * times, times)], head_send.at[s - 1],
                      head_recv.at[s - 1], {"row": lax.rem(row + s, row_n)})

    def finish(c):
        for s in range(row_n):
            out_copy(c, s).wait()

    def split(c):
        if c >= count:
            return
        in_copy(c).wait()
        if c + 1 < count:
            in_copy(c + 1).start()
        if c >= 2:
            finish(c - 2)
        for k in range(row_n):
            @pl.when(row == k)
            def _():
                def strip(t, carry):
                    at = pl.ds(pl.multiple_of(lax.rem(t, times // 16) * 16, 16), 16)
                    cut = pl.ds(pl.multiple_of(t // (times // 16) * sizes[0], sizes[0]), sizes[0])
                    for s in range(row_n):
                        sorted_[c % 2, s, at, cut] = source[c % 2, at, (k + s) % row_n, cut]
                    return carry

                lax.fori_loop(0, times // 16 * (sizes[c] // sizes[0]), strip, 0)
        for s in range(row_n):
            out_copy(c, s).start()

    started = []

    def start(copy):
        copy.start()
        started.append(copy)

    in_copy(0).start()
    for h in range(2):
        for d in range(1, plane):
            start(sum_copy(h, d))
    for d in range(1, col_n):
        start(ridge_copy(d))
    ridges[col] = ridge[...]
    split(0)
    for h in range(2):
        total = part[:, columns(me, h)].astype(jnp.float32)
        for d in range(1, plane):
            sum_copy(h, d).wait_recv()
            total = total + summed[h, d - 1].astype(jnp.float32)
        series[h, here] = total.astype(jnp.bfloat16)
        for d in range(1, row_n):
            start(row_copy(h, d))
    split(1)
    split(2)
    for h in range(2):
        for d in range(1, row_n):
            row_copy(h, d).wait_recv()
        out[:, columns(me, h)] = mm(w[...], series[h]).astype(jnp.bfloat16)
        for e in range(1, len(steps)):
            start(far_copy(h, e))
        start(near_copy(h, 0))
    if count < 3:
        finish(0)
    for s in range(1, row_n):
        start(head_copy(s))
    split(3)
    split(4)
    split(5)
    for h in range(2):
        for e in range(1, len(steps)):
            far_copy(h, e).wait_recv()
            start(near_copy(h, e))
    for d in range(1, col_n):
        ridge_copy(d).wait_recv()
    for h in range(2):
        for e in range(len(steps)):
            near_copy(h, e).wait_recv()
    for c in range(max(count - 2, 1 if count < 3 else 0), count):
        finish(c)
    for s in range(1, row_n):
        head_copy(s).wait_recv()
    for copy in started:
        copy.wait_send()


def gather_slab(part, ridge, w, flat, starts, sizes, row_n, col_n, tm_n):
    times, slab = part.shape
    depth = w.shape[0]
    plane = col_n * tm_n
    wide = slab // plane // 2
    far = col_n // 2 * tm_n
    dma = pltpu.SemaphoreType.DMA
    vmem = pl.BlockSpec(memory_space=pltpu.VMEM)
    return pl.pallas_call(
        functools.partial(gather_kernel, row_n, col_n, tm_n, starts, sizes),
        out_shape=[jax.ShapeDtypeStruct((depth, slab), jnp.bfloat16),
                   jax.ShapeDtypeStruct((col_n,) + ridge.shape, jnp.float32),
                   jax.ShapeDtypeStruct((times, flat.shape[2]), flat.dtype),
                   jax.ShapeDtypeStruct(((row_n - 1) * times, sizes[0]), flat.dtype)]
        + [jax.ShapeDtypeStruct((times, n), flat.dtype) for n in sizes for _ in range(row_n - 1)],
        in_specs=[vmem] * 3 + [pl.BlockSpec(memory_space=pl.ANY)],
        out_specs=[vmem] * 2 + [pl.BlockSpec(memory_space=pl.ANY)] * (2 + len(sizes) * (row_n - 1)),
        scratch_shapes=[
            pltpu.VMEM((2, plane - 1, times, wide), jnp.bfloat16),
            pltpu.VMEM((2, depth, wide), jnp.bfloat16),
            pltpu.VMEM((2, times, row_n, max(sizes)), jnp.bfloat16),
            pltpu.VMEM((2, row_n, times, max(sizes)), jnp.bfloat16),
            dma((2, plane - 1)), dma((2, plane - 1)), dma((2, row_n - 1)), dma((2, row_n - 1)),
            dma((2, far - 1)), dma((2, far - 1)), dma((2, far)), dma((2, far)),
            dma((col_n - 1,)), dma((col_n - 1,)),
            dma((2,)), dma((2, row_n)), dma((row_n - 1,)), dma((row_n - 1,)),
        ],
        compiler_params=pltpu.CompilerParams(
            collective_id=1, has_side_effects=True, vmem_limit_bytes=60 * 2**20),
        cost_estimate=pl.CostEstimate(flops=40 * 10**9, bytes_accessed=2**20, transcendentals=0),
        name="gather_slab",
    )(part, ridge, w, flat)


def pick_kernel(rows, info, x_ref, o_ref):
    keep = info[1 + pl.program_id(0)] > 0
    for k in range(rows):
        @pl.when(keep & (info[0] == k))
        def _():
            def strip(t, carry):
                at = pl.ds(pl.multiple_of(t * 16, 16), 16)
                o_ref[at, :] = x_ref[at, k, :]
                return carry

            lax.fori_loop(0, o_ref.shape[0] // 16, strip, 0)

    @pl.when(jnp.logical_not(keep))
    def _():
        o_ref[...] = jnp.zeros_like(o_ref)


def pick_blocks(which, keep, at, x, wide):
    times, rows, _ = x.shape
    n = at.shape[0]
    info = jnp.concatenate([which.reshape(1), keep, at]).astype(jnp.int32)
    return pl.pallas_call(
        functools.partial(pick_kernel, rows),
        grid_spec=pltpu.PrefetchScalarGridSpec(
            num_scalar_prefetch=1,
            grid=(n,),
            in_specs=[pl.BlockSpec((times, rows, wide), lambda p, info: (0, 0, info[1 + n + p]))],
            out_specs=pl.BlockSpec((times, wide), lambda p, info: (0, p)),
        ),
        out_shape=jax.ShapeDtypeStruct((times, n * wide), x.dtype),
        cost_estimate=pl.CostEstimate(flops=0, bytes_accessed=2 * times * rows * n * wide * 2, transcendentals=0),
        name="pick_blocks",
    )(info, x)


def final_body(chunk_base, units, per, start, info, *refs):
    owns, others = refs[:units], refs[units:2 * units]
    p_ref, d_ref, r_ref = refs[2 * units:2 * units + 3]
    t_ref, f_ref, held, arrived = refs[-4:]
    bm, width = t_ref.shape
    times = owns[0].shape[0]
    step = pl.program_id(0) * per + pl.program_id(1)
    slot = step % 2

    def copies(u, i, slot):
        return (
            pltpu.make_async_copy(
                owns[u].at[:, pl.ds(pl.multiple_of(start + i * bm, bm), bm)], held.at[slot, pl.ds(0, times)],
                arrived.at[slot, 0]),
            pltpu.make_async_copy(
                others[u].at[:, pl.ds(pl.multiple_of(i * bm, bm), bm)],
                held.at[slot, pl.ds(times, held.shape[1] - times)], arrived.at[slot, 1]),
        )

    def fetch(n):
        for u in range(units):
            @pl.when(n // per == u)
            def _():
                for copy in copies(u, n % per, n % 2):
                    copy.start()

    @pl.when(step == 0)
    def _():
        fetch(step)

    @pl.when(step + 1 < units * per)
    def _():
        fetch(step + 1)

    for copy in copies(0, 0, slot):
        copy.wait()
    acc = mm(held[slot], p_ref[...], TN)
    kind = kind_of(info, chunk_base(pl.program_id(0), pl.program_id(1), info))

    def put(first, second, last):
        f_ref[0] = first.astype(f_ref.dtype)
        f_ref[1] = second.astype(f_ref.dtype)
        t_ref[...] = last

    @pl.when(kind < 2)
    def _():
        full = acc + d_ref[...]
        put(full[:, :width], full[:, width:2 * width], full[:, 2 * width:])

    @pl.when(kind == 2)
    def _():
        put(acc[:, :width], acc[:, width:2 * width],
            acc[:, 2 * width:] + jnp.where(eye_mask(width), r_ref[...], 0.0))

    @pl.when(kind > 2)
    def _():
        put(acc[:, :width], acc[:, width:2 * width], acc[:, 2 * width:])


def kind_of(info, block):
    at = block - info[4]
    inside = (at >= 0) & (at < info[5])
    kind = jnp.where(at == info[0], 0, jnp.where(at == info[1], 1, jnp.where(at == info[2], 2, 3)))
    return jnp.where(inside, kind, 3)


def final_chunk(info, own, others, weights, d, ridge, prior, start, width):
    units = len(others)
    times, local = own[0].shape
    rest, w = others[0].shape
    bm = width
    per = w // bm
    rows = units * local

    def base(c, i, info):
        far, bits = 0, units.bit_length() - 1
        for b in range(bits):
            far = far + (((c >> b) & 1) << (bits - 1 - b))
        return (info[2] ^ far) * (local // bm) + start // bm + i

    in_specs = [pl.BlockSpec(memory_space=pl.ANY)] * (2 * units) + [
        pl.BlockSpec(weights.shape, lambda c, i, info: (0, 0)),
        pl.BlockSpec((bm, 3 * width), lambda c, i, info: (jnp.where(kind_of(info, base(c, i, info)) == 1, 1, 0), 0)),
        pl.BlockSpec((1, width), lambda c, i, info: (0, 0)),
    ]
    operands = [info, *own, *others, weights, d, ridge]
    aliases = {}
    if prior is not None:
        in_specs += [pl.BlockSpec(memory_space=pl.ANY)] * 2
        aliases = {len(operands): 0, len(operands) + 1: 1}
        operands += list(prior)
    return pl.pallas_call(
        functools.partial(final_body, base, units, per, start),
        grid_spec=pltpu.PrefetchScalarGridSpec(
            num_scalar_prefetch=1,
            grid=(units, per),
            in_specs=in_specs,
            out_specs=[
                pl.BlockSpec((bm, width), lambda c, i, info: (base(c, i, info), 0)),
                pl.BlockSpec((2, bm, width), lambda c, i, info: (0, base(c, i, info), 0)),
            ],
            scratch_shapes=[pltpu.VMEM((2, times + rest, bm), jnp.bfloat16), pltpu.SemaphoreType.DMA((2, 2))],
        ),
        out_shape=[
            jax.ShapeDtypeStruct((rows, width), jnp.float32),
            jax.ShapeDtypeStruct((2, rows, width), jnp.bfloat16),
        ],
        input_output_aliases=aliases,
        compiler_params=pltpu.CompilerParams(
            vmem_limit_bytes=48 * 2**20, dimension_semantics=("arbitrary", "arbitrary")
        ),
        cost_estimate=pl.CostEstimate(
            flops=2 * units * w * (times + rest) * 3 * width, bytes_accessed=units * w * 6 * 2**10, transcendentals=0),
        name="final",
    )(*operands)


def hop_gather(block, cols):
    held = [block]
    bit = cols // 2
    while bit:
        moved = []
        for h in held:
            moved.append(lax.ppermute(h, "col", [(i, i ^ bit) for i in range(cols)]))
        held = held + moved
        bit //= 2
    return held


def on_device(samples, whitening, ridge, slab_start, panels):
    times, groups, _, local = samples.shape
    rows = lax.axis_size("row")
    cols = lax.axis_size("col")
    tms = lax.axis_size("tm")
    width = ridge.shape[0]
    slab = width * cols
    kd = local * cols
    depth = whitening.shape[0]
    scale = 1.0 / math.sqrt(depth)
    me_col = lax.axis_index("col")
    me_tm = lax.axis_index("tm")
    me_row = lax.axis_index("row")

    first = slab_start[0] * slab
    group = first // (tms * kd)
    tm_owner = (first % (tms * kd)) // kd
    offset = first % kd

    flat = samples.reshape(times, groups, local)
    eighth = local // 8
    sizes = [eighth * n for n in (1, 2, 2, 1, 1, 1)] if eighth >= width else [width] * (local // width)
    starts = [sum(sizes[:c]) for c in range(len(sizes))]
    at = offset + jnp.arange(cols) * width
    have = (me_tm == tm_owner) & (me_col == at // local)
    part = pick_blocks(group, have, at % local // width, flat, width)
    sw, ridges, own, head, *pieces = gather_slab(
        part, jnp.broadcast_to(ridge, (SUB, width)), whitening, flat, starts, sizes, rows, cols, tms)
    ridges = ridges[:, 0].reshape(1, slab)
    own = hop_gather(own, cols)
    others = []
    for c in range(len(sizes)):
        block = pieces[c * (rows - 1):(c + 1) * (rows - 1)]
        if c:
            head = jnp.concatenate([
                lax.ppermute(block[s - 1], "row", [(i, (i + s) % rows) for i in range(rows)])
                for s in range(1, rows)
            ], axis=0)
        others.append(hop_gather(head, cols))

    q0, q1 = panels[0], panels[1]
    owner = (me_row == group) & (me_tm == tm_owner)
    kind = jnp.where(me_col == q0, 0, jnp.where(me_col == q1, 1, 2))
    info = jnp.stack([
        q0, q1, me_col, kind, offset // width, jnp.where(owner, cols, 0), me_row,
    ]).astype(jnp.int32)
    square = jax.ShapeDtypeStruct((width, width), jnp.float32)
    coarse = jax.ShapeDtypeStruct((width, width), jnp.bfloat16)
    scratch = [pltpu.VMEM((width, 2 * width), jnp.float32), pltpu.VMEM((NB, 2 * width), jnp.float32),
               pltpu.VMEM((2, NB // SUB, SUB, SUB, NB), jnp.float32)]
    i0, = chain_call(
        functools.partial(first_kernel, scale), info, [sw, ridges], [0, 0], [square], scratch, 20 * 10**9, "first")
    c01, c0j, i1 = chain_call(
        functools.partial(second_kernel, scale), info, [sw, sw, sw, ridges, ridges, i0], [0, 1, 2, 0, 1, None],
        [coarse, coarse, square], scratch, 24 * 10**9, "second")
    weights, d = chain_call(
        functools.partial(third_kernel, scale, rows), info,
        [sw, sw, sw, ridges, ridges, i0, i1, c01, c0j, whitening], [0, 1, 2, 0, 1, None, None, None, None, None],
        [jax.ShapeDtypeStruct((depth, 3 * width), jnp.bfloat16), jax.ShapeDtypeStruct((2 * width, 3 * width), jnp.float32)],
        [pltpu.VMEM((width, width), jnp.bfloat16)], 15 * 10**9, "third")
    own_ridge = ridge.reshape(1, width) * (kind == 2).astype(jnp.float32)

    prior = None
    for c, start in enumerate(starts):
        prior = final_chunk(info, own, others[c], weights, d, own_ridge, prior, start, width)
    return tuple(prior)


def solution(mesh):
    in_specs = (P("row", None, "tm", "col"), P(), P("col"), P(), P())
    out_specs = (P(("row", "tm"), "col"), P(None, ("row", "tm"), None))
    return jax.shard_map(on_device, mesh=mesh, in_specs=in_specs, out_specs=out_specs, check_vma=False)
```
